256 devices in a mesh: dp: 4 (over y), expert: 64 (over x, z, core).
Axes of the slice: x: 4, y: 4, z: 8, core: 2. Of those that a mesh axis runs over, the one named last changes fastest.
Arguments:
- tokens: bfloat16 [8192, 2048], P(('dp', 'expert')), may hold values from -6 to 6
- grad_out: bfloat16 [8192, 2048], P(('dp', 'expert')), may hold values from -1.5 to 1.5
- expert_ids: int32 [8192, 8], P(('dp', 'expert')), may hold values from 0 to 63, all different within a row; in each aligned block of 32 rows (0 to 31, 32 to 63, ...) at most 6 rows name the same one
- gate_values: bfloat16 [8192, 8], P(('dp', 'expert')), may hold values from 0.099609375 to 1
- w_gate: bfloat16 [64, 2048, 768], P('expert'), may hold values from -0.125 to 0.125
- w_up: bfloat16 [64, 2048, 768], P('expert'), may hold values from -0.125 to 0.125
- w_down: bfloat16 [64, 768, 2048], P('expert'), may hold values from -0.21875 to 0.21875
Outputs:
- token_grad: bfloat16 [8192, 2048], P(('dp', 'expert'))
- gate_grad: bfloat16 [8192, 8], P(('dp', 'expert'))
- gate_weight_grad: bfloat16 [64, 2048, 768], P('expert', 'dp')
- up_weight_grad: bfloat16 [64, 2048, 768], P('expert', 'dp')
- down_weight_grad: bfloat16 [64, 768, 2048], P('expert', 'dp')
The draws below stay inside these ranges and needn't reach their ends.
Inputs may be any that keep to these rules, and one draw needn't show every extreme that they name: `expert_ids`: each token names 8 different experts. Within the 32 rows of one device no expert is named more than 6 times, and some device names some expert exactly 6 times.
All inputs are finite; a program needn't handle non-finite values.
Results may differ from the reference program's by a relative error of at most 0.015.
Values may be sent and summed in bfloat16 or wider, within the bound.
No kernel may reach another device: no remote copies, remote signals or barrier semaphores. Data moves between devices by JAX's collectives and lax.ppermute only.
A program may use at most 128 MiB of HBM per device.

```python
import math
import jax
import jax.numpy as jnp
import numpy as np
from jax import lax

D = 2048
FF = 768
TOPK = 8
TOK_DEV = 32
EXPERTS = 64
CAP = 6
TOKENS = 8192
N_DP = 4
N_EXPERT = 64


def shard_levels(stream_key, shape, split, smallest, top_value):
    factor_of = 1.0
    for dim, blocks in split:
        steps = jax.random.uniform(jax.random.fold_in(jax.random.fold_in(stream_key, 6), dim), (blocks,), jnp.float32, smallest / len(split), top_value / len(split))
        factor_of = factor_of * jnp.repeat(jnp.exp(steps), shape[dim] // blocks).reshape((-1,) + (1,) * (len(shape) - 1 - dim))
    return factor_of


def deal_out(rng, own, number, rows, number_of, top, most, slope):
    order = jax.random.permutation(rng, number_of)
    packed, common = load_shares(number_of, rows * top, most, slope, True), load_shares(number_of, rows * top, most, slope, False)
    places = jnp.arange(number_of)

    def named(lengths, rotation):
        used = int((lengths > 0).sum())
        fixed = max(1, used // 4)
        moved = fixed + (places - fixed + rotation * (used - fixed)) % max(1, number_of - fixed)
        return jnp.zeros((number_of,), jnp.int32).at[order[jnp.where(places < fixed, places, moved)]].set(jnp.asarray(lengths, jnp.int32))

    lengths = jnp.where(number % 4 == 0, named(packed, number // 4), named(common, number - number // 4 - 1))
    mixed = jax.random.permutation(jax.random.fold_in(own, 3), number_of)
    donor, sink = mixed[0:number_of // 2 * 2:2], mixed[1:number_of // 2 * 2:2]
    margin = jnp.minimum(lengths[donor] - 1, most - lengths[sink]) // 2
    margin = jnp.where((donor == order[0]) | (sink == order[0]) | (lengths[sink] == 0), 0, jnp.maximum(margin, 0))
    moved = jax.random.randint(jax.random.fold_in(own, 4), (number_of // 2,), 0, 1 << 20) % (margin + 1)
    lengths = lengths.at[donor].add(-moved).at[sink].add(moved)
    members = jnp.searchsorted(jnp.cumsum(lengths), jnp.arange(rows * top), side="right").astype(jnp.int32)
    table = members.reshape(top, rows).T
    table = table[jax.random.permutation(jax.random.fold_in(own, 1), rows)]
    rotation = jax.random.randint(jax.random.fold_in(own, 2), (rows, 1), 0, top)
    return jnp.take_along_axis(table, (jnp.arange(top)[None, :] + rotation) % top, axis=1)


def load_shares(count, total, reach, lean, full):
    weights = [(1 << 20) // math.isqrt(grade ** lean) + 1 for grade in range(1, count + 1)]
    largest = reach if full else min(reach, max(-(-total // count), total * weights[0] // sum(weights)))
    least = 1 if total - largest >= count - 1 else 0
    counts, surplus = [largest] + [least] * (count - 1), total - largest - least * (count - 1)
    while surplus > 0:
        candidates = [i for i in range(1, count) if counts[i] < largest] or [i for i in range(1, count) if counts[i] < reach]
        mass, remaining = sum([weights[i] for i in candidates]), surplus
        for i in candidates:
            extra = min(reach - counts[i], max(1, remaining * weights[i] // mass), surplus)
            counts[i] = counts[i] + extra
            surplus = surplus - extra
    return np.array(counts)


def scatter_about(rng, shape, scale, reach, split=(), kind=jnp.bfloat16):
    entries = jax.random.normal(rng, shape, jnp.float32) * scale
    if len(split) > 0:
        entries = shard_levels(rng, shape, split, -0.22, 0.18) * entries
    return jnp.clip(entries, min=-reach, max=reach).astype(kind)


def setup_inputs(seed: int = 0) -> dict:
    arg_keys = jax.random.split(jax.random.key(seed), 8)
    tokens = scatter_about(arg_keys[0], (TOKENS, D), 1.0, 6.0, ((0, 256),))
    grad_out = scatter_about(arg_keys[1], (TOKENS, D), 0.25, 1.5, ((0, 256),))
    expert_ids_keys = jax.random.split(jax.random.fold_in(arg_keys[2], 1), TOKENS // TOK_DEV)
    expert_ids_turns = jax.random.permutation(jax.random.fold_in(arg_keys[2], 3), TOKENS // TOK_DEV)
    expert_ids = jax.vmap(lambda own, number: deal_out(jax.random.fold_in(arg_keys[2], 2), own, number, TOK_DEV, EXPERTS, TOPK, CAP, 2))(expert_ids_keys, expert_ids_turns).reshape((TOKENS, TOPK))
    gate_values = jnp.clip(jnp.exp(math.log(1.0) - 2.306499 * jax.random.uniform(arg_keys[3], (TOKENS, TOPK), jnp.float32) ** shard_levels(arg_keys[3], (TOKENS, TOPK), ((0, 256),), -0.2, 0.2)), 0.099609375, 1.0).astype(jnp.bfloat16)
    w_gate = scatter_about(arg_keys[4], (EXPERTS, D, FF), D ** -0.5, 0.125, ((0, 64),))
    w_up = scatter_about(arg_keys[5], (EXPERTS, D, FF), D ** -0.5, 0.125, ((0, 64),))
    w_down = scatter_about(arg_keys[6], (EXPERTS, FF, D), FF ** -0.5, 0.21875, ((0, 64),))
    return dict(tokens=tokens, grad_out=grad_out, expert_ids=expert_ids, gate_values=gate_values, w_gate=w_gate, w_up=w_up, w_down=w_down)


def reference(tokens, grad_out, expert_ids, gate_values, w_gate, w_up, w_down):
    copies_dev = TOK_DEV * TOPK
    blocks = TOKENS // TOK_DEV
    total_rows = blocks * CAP
    ids_block = expert_ids.reshape(blocks, copies_dev)
    onehot = (ids_block[:, :, None] == jnp.arange(EXPERTS, dtype=jnp.int32)[None, None, :]).astype(jnp.int32)
    earlier = jnp.cumsum(onehot, axis=1) - onehot
    slot_pos = jnp.sum(earlier * onehot, axis=2)
    rowpos = (jnp.arange(blocks, dtype=jnp.int32)[:, None] * CAP + slot_pos).reshape(-1).astype(jnp.int32)
    flat_ids = expert_ids.reshape(-1)
    copy_index = jnp.arange(TOKENS * TOPK, dtype=jnp.int32)

    def per_expert(totals, inputs):
        expert_num, gate_matrix, up_matrix, down_matrix = inputs
        token_sum, gate_sum = totals
        chosen = flat_ids == expert_num
        where_row = jnp.where(chosen, rowpos, total_rows).astype(jnp.int32)
        owner = jnp.full((total_rows,), -1, jnp.int32).at[where_row].set(copy_index, mode="drop")
        filled = owner >= 0
        owner_safe = jnp.maximum(owner, 0)
        token_index = owner_safe // TOPK
        pick_index = owner_safe % TOPK
        zero_bf = jnp.zeros((), jnp.bfloat16)
        x_rows = jnp.where(filled[:, None], tokens[token_index], zero_bf)
        dy_rows = jnp.where(filled[:, None], grad_out[token_index], zero_bf)
        gate_rows = jnp.where(filled, gate_values[token_index, pick_index].astype(jnp.float32), jnp.float32(0.0))
        gate_pre = jnp.dot(x_rows, gate_matrix, preferred_element_type=jnp.float32)
        up_pre = jnp.dot(x_rows, up_matrix, preferred_element_type=jnp.float32)
        sigmoid_gate = jax.nn.sigmoid(gate_pre)
        swish = gate_pre * sigmoid_gate
        hidden = (swish * up_pre).astype(jnp.bfloat16)
        output = jnp.dot(hidden, down_matrix, preferred_element_type=jnp.float32)
        row_gate = jnp.sum(dy_rows.astype(jnp.float32) * output, axis=1).astype(jnp.bfloat16)
        scaled = (gate_rows[:, None] * dy_rows.astype(jnp.float32)).astype(jnp.bfloat16)
        grad_hidden = jnp.dot(scaled, down_matrix.T, preferred_element_type=jnp.float32)
        grad_a = (grad_hidden * up_pre * sigmoid_gate * (1.0 + gate_pre * (1.0 - sigmoid_gate))).astype(jnp.bfloat16)
        grad_u = (grad_hidden * swish).astype(jnp.bfloat16)
        row_grad = (jnp.dot(grad_a, gate_matrix.T, preferred_element_type=jnp.float32)
                    + jnp.dot(grad_u, up_matrix.T, preferred_element_type=jnp.float32)).astype(jnp.bfloat16)
        token_sum = token_sum.at[token_index].add(jnp.where(filled[:, None], row_grad.astype(jnp.float32), jnp.float32(0.0)))
        gate_sum = gate_sum.at[token_index, pick_index].add(jnp.where(filled, row_gate.astype(jnp.float32), jnp.float32(0.0)))
        group_rows = N_EXPERT * CAP
        x_group = x_rows.reshape(N_DP, group_rows, D).astype(jnp.float32)
        ga_group = grad_a.reshape(N_DP, group_rows, FF).astype(jnp.float32)
        gu_group = grad_u.reshape(N_DP, group_rows, FF).astype(jnp.float32)
        h_group = hidden.reshape(N_DP, group_rows, FF).astype(jnp.float32)
        s_group = scaled.reshape(N_DP, group_rows, D).astype(jnp.float32)
        part_gate = jnp.einsum("grd,grf->gdf", x_group, ga_group).astype(jnp.bfloat16).astype(jnp.float32)
        part_up = jnp.einsum("grd,grf->gdf", x_group, gu_group).astype(jnp.bfloat16).astype(jnp.float32)
        part_down = jnp.einsum("grf,grd->gfd", h_group, s_group).astype(jnp.bfloat16).astype(jnp.float32)
        grads = (jnp.sum(part_gate, axis=0).astype(jnp.bfloat16),
                 jnp.sum(part_up, axis=0).astype(jnp.bfloat16),
                 jnp.sum(part_down, axis=0).astype(jnp.bfloat16))
        return (token_sum, gate_sum), grads

    start_totals = (jnp.zeros((TOKENS, D), jnp.float32), jnp.zeros((TOKENS, TOPK), jnp.float32))
    (token_sum, gate_sum), (grad_gate_w, grad_up_w, grad_down_w) = lax.scan(
        per_expert, start_totals, (jnp.arange(EXPERTS, dtype=jnp.int32), w_gate, w_up, w_down))
    return (token_sum.astype(jnp.bfloat16), gate_sum.astype(jnp.bfloat16), grad_gate_w, grad_up_w, grad_down_w)
```

```python
import jax
import jax.numpy as jnp
from jax import lax
from jax.sharding import Mesh
from jax.sharding import PartitionSpec as P

BF = jnp.bfloat16
F32 = jnp.float32
AXES = ("dp", "x", "z", "c")
TOP_K = 8
CAP = 6
NZ = 8
NXC = 8
EXT = 128


def dot(a, b, dims):
    return lax.dot_general(a, b, (dims, ((), ())), preferred_element_type=F32)


def z_columns(payload):
    up = [(i, (i + 1) % NZ) for i in range(NZ)]
    down = [(i, (i - 1) % NZ) for i in range(NZ)]
    half = payload.shape[1] // 256 * 128
    above, below = [], []
    a = b = payload
    for _ in range(3):
        a = lax.ppermute(a, "z", down)
        b = lax.ppermute(b, "z", up)
        above.append(a)
        below.append(b)
    far_a = lax.ppermute(a[:, :half], "z", down)
    far_b = lax.ppermute(b[:, half:], "z", up)
    far = jnp.concatenate([far_a, far_b], axis=1)
    return jnp.concatenate([payload] + above + [far] + below[::-1], axis=0)


def swap(v, order):
    pairs = [(0, 1), (1, 0), (2, 3), (3, 2)] if order == 1 else [(0, 3), (3, 0), (1, 2), (2, 1)]
    return lax.ppermute(v, "dp", pairs)


def per_device(tokens, grad_out, expert_ids, gate_values, w_gate, w_up, w_down):
    tok_dev, features = tokens.shape
    hidden_units = w_gate.shape[2]
    experts = NZ * NXC
    g, xi, zi, ci = (lax.axis_index(name) for name in AXES)
    me = xi * 16 + zi * 2 + ci
    wg, wu, wd = w_gate[0], w_up[0], w_down[0]
    rows = experts * CAP

    named = expert_ids[:, :, None] == jnp.arange(experts, dtype=jnp.int32)[None, None, :]
    chosen = jnp.any(named, axis=1)
    before = (jnp.arange(tok_dev)[:, None] > jnp.arange(tok_dev)[None, :]).astype(BF)
    slot = dot(before, chosen.astype(BF), ((1,), (0,)))
    code = jnp.where(chosen, slot + 1.0, 0.0).astype(BF)
    gate_of = jnp.sum(jnp.where(named, gate_values[:, :, None].astype(F32), 0.0), axis=1).astype(BF)
    payload = jnp.concatenate([tokens, grad_out, code, gate_of], axis=1)
    column = z_columns(payload)
    col_x = column[:, :features]
    col_dy = column[:, features : 2 * features]
    col_code = column[:, 2 * features : 2 * features + experts]
    col_gate = column[:, 2 * features + experts :]

    r = jnp.arange(rows, dtype=jnp.int32)
    dest = r // (NZ * CAP)
    block = (r // CAP) % NZ
    want = (r % CAP + 1).astype(F32)
    expert = (dest // 2) * 16 + zi * 2 + dest % 2
    pick_expert = (expert[:, None] == jnp.arange(experts, dtype=jnp.int32)[None, :]).astype(BF)
    t_block = jnp.arange(NZ * tok_dev, dtype=jnp.int32) // tok_dev
    code_rt = dot(pick_expert, col_code, ((1,), (1,)))
    gate_rt = dot(pick_expert, col_gate, ((1,), (1,)))
    hit = (code_rt == want[:, None]) & (block[:, None] == t_block[None, :])
    picked = hit.astype(BF)
    weighted = jnp.where(hit, gate_rt, 0.0).astype(BF)
    sent_x = dot(picked, col_x, ((1,), (0,))).astype(BF).reshape(NXC, NZ * CAP, features)
    sent_s = dot(weighted, col_dy, ((1,), (0,))).astype(BF).reshape(NXC, NZ * CAP, features)
    sent = jnp.concatenate([sent_x, sent_s], axis=1)
    got = lax.all_to_all(sent, ("x", "c"), split_axis=0, concat_axis=0, tiled=True)
    x_rows = got[:, : NZ * CAP].reshape(rows, features)
    scaled = got[:, NZ * CAP :].reshape(rows, features)

    a = dot(x_rows, wg, ((1,), (0,)))
    u = dot(x_rows, wu, ((1,), (0,)))
    gh = dot(scaled, wd, ((1,), (1,)))
    sig = jax.nn.sigmoid(a)
    swish = a * sig
    hidden = (swish * u).astype(BF)
    ga = (gh * u * sig * (1.0 + a * (1.0 - sig))).astype(BF)
    gu = (gh * swish).astype(BF)
    row_gate = jnp.sum(gh * hidden.astype(F32), axis=1)

    dq = features // 4
    fq = hidden_units // 4
    hd = features // 2
    s_left, s_right = scaled[:, :hd], scaled[:, hd:]

    def x_part(q, ct):
        return dot(lax.dynamic_slice_in_dim(x_rows, q * dq, dq, 1), ct, ((0,), (0,)))

    def h_part(q, s):
        return dot(lax.dynamic_slice_in_dim(hidden, q * fq, fq, 1), s, ((0,), (0,)))

    def quarter(q, first):
        if first:
            return x_part(q, ga), h_part(q, s_left)
        return x_part(q, gu), h_part(q, s_right)

    far = g ^ 2
    sends = []
    for first, near in ((True, g ^ 1), (False, g ^ 3)):
        w_near, d_near = quarter(near, first)
        w_far, d_far = quarter(far, first)
        sends.append(
            (
                jnp.concatenate([w_near, w_far], 0).astype(BF),
                jnp.concatenate([d_near, d_far], 0).astype(BF),
            )
        )
    (a_w, a_d), (b_w, b_d) = sends
    ra_w, rb_w = swap(a_w, 1), swap(b_w, 3)
    ra_d, rb_d = swap(a_d, 1), swap(b_d, 3)

    row_grad = (dot(ga, wg, ((1,), (1,))) + dot(gu, wu, ((1,), (1,)))).astype(BF)
    gate_block = jnp.where(
        jnp.arange(EXT, dtype=jnp.int32)[None, :] == me, row_gate[:, None], 0.0
    ).astype(BF)
    back = jnp.concatenate([row_grad, gate_block], axis=1).reshape(NXC, NZ * CAP, features + EXT)
    back = lax.all_to_all(back, ("x", "c"), split_axis=0, concat_axis=0, tiled=True)
    back = back.reshape(rows, features + EXT)

    a_own, ad_own = quarter(g, True)
    a_next, ad_next = quarter(g ^ 3, True)
    b_own, bd_own = quarter(g, False)
    b_next, bd_next = quarter(g ^ 1, False)
    a_next = (a_next + ra_w[dq:].astype(F32)).astype(BF)
    ad_next = (ad_next + ra_d[fq:].astype(F32)).astype(BF)
    b_next = (b_next + rb_w[dq:].astype(F32)).astype(BF)
    bd_next = (bd_next + rb_d[fq:].astype(F32)).astype(BF)
    sa_w, sb_w = swap(a_next, 3), swap(b_next, 1)
    sa_d, sb_d = swap(ad_next, 3), swap(bd_next, 1)
    gate_weight_grad = (a_own + ra_w[:dq].astype(F32) + sa_w.astype(F32)).astype(BF)
    up_weight_grad = (b_own + rb_w[:dq].astype(F32) + sb_w.astype(F32)).astype(BF)
    down_l = (ad_own + ra_d[:fq].astype(F32) + sa_d.astype(F32)).astype(BF)
    down_r = (bd_own + rb_d[:fq].astype(F32) + sb_d.astype(F32)).astype(BF)
    down_weight_grad = jnp.concatenate([down_l, down_r], axis=1)

    twice = jnp.concatenate([col_code, col_code], axis=0)
    abs_code = lax.dynamic_slice_in_dim(twice, ((NZ - zi) % NZ) * tok_dev, NZ * tok_dev, 0)
    abs_block = (t_block - zi) % NZ
    abs_rt = dot(pick_expert, abs_code, ((1,), (1,)))
    abs_hit = ((abs_rt == want[:, None]) & (block[:, None] == abs_block[None, :])).astype(BF)
    summed = dot(abs_hit, back, ((0,), (0,))).astype(BF).reshape(NZ, tok_dev, features + EXT)
    summed = lax.all_to_all(summed, "z", split_axis=0, concat_axis=0, tiled=True)
    total = jnp.sum(summed.astype(F32), axis=0)
    token_grad = total[:, :features].astype(BF)
    gate_cols = total[:, features : features + experts]
    gate_grad = jnp.sum(jnp.where(named, gate_cols[:, None, :], 0.0), axis=2)
    gate_grad = (gate_grad / gate_values.astype(F32)).astype(BF)
    return (
        token_grad,
        gate_grad,
        gate_weight_grad[None],
        up_weight_grad[None],
        down_weight_grad[None],
    )


def solution(mesh):
    inner = Mesh(mesh.devices.reshape(4, 4, 8, 2), AXES)
    tok = P(AXES, None)
    weight = P(("x", "z", "c"), None, None)
    grad = P(("x", "z", "c"), "dp", None)
    return jax.shard_map(
        per_device,
        mesh=inner,
        in_specs=(tok, tok, tok, tok, weight, weight, weight),
        out_specs=(tok, tok, grad, grad, grad),
        check_vma=False,
    )
```

```python
import jax
import jax.numpy as jnp
from jax import lax
from jax.experimental import pallas as pl
from jax.experimental.pallas import tpu as pltpu
from jax.sharding import Mesh
from jax.sharding import PartitionSpec as P

BF = jnp.bfloat16
F32 = jnp.float32
I32 = jnp.int32
AXES = ("dp", "x", "z", "c")
CAP = 6
NX = 4
NZ = 8
EXPERTS = 64
EXT = 128
OFFSETS = [(dx, dc) for dx in (0, 1, 3, 2) for dc in (0, 1)]
N_OFF = len(OFFSETS)
WAVE = 4
ROWS_W = WAVE * CAP
MIB = 1 << 20
VMEM_SPEC = pl.BlockSpec(memory_space=pltpu.VMEM)
SMEM_SPEC = pl.BlockSpec(memory_space=pltpu.SMEM)


def dot(a, b, dims):
    return lax.dot_general(a, b, (dims, ((), ())), preferred_element_type=F32)


def cost(flops, nbytes):
    return pl.CostEstimate(flops=flops, bytes_accessed=nbytes, transcendentals=0)


def expert_of(off, xi, zi, ci):
    half = off >> 1
    dx = half ^ (half >> 1)
    return ((xi + dx) & (NX - 1)) * (2 * NZ) + zi * 2 + (ci ^ (off & 1))


def select_kernel(place, b0, b1, b2, b3, *outs):
    xi, zi, ci = place[0], place[1], place[2]
    blocks = (b0, b1, b2, b3)
    tok = b0.shape[0]
    d = (b0.shape[1] - EXT) // 2
    rows = N_OFF * ROWS_W
    ext = jnp.concatenate([b[:, 2 * d :] for b in blocks], axis=0)
    r = lax.broadcasted_iota(I32, (rows, EXT), 0)
    col = lax.broadcasted_iota(I32, (rows, EXT), 1)
    off = (r * 2731) >> 16
    expert = expert_of(off, xi, zi, ci)
    code = dot((col == expert).astype(F32).astype(BF), ext, ((1,), (1,)))
    gate = dot((col == expert + EXPERTS).astype(F32).astype(BF), ext, ((1,), (1,)))
    n_tok = WAVE * tok
    r = lax.broadcasted_iota(I32, (rows, n_tok), 0)
    t = lax.broadcasted_iota(I32, (rows, n_tok), 1)
    m = r - ((r * 2731) >> 16) * ROWS_W
    block = (m * 10923) >> 16
    slot = m - block * CAP
    hit = (code == (slot + 1).astype(F32)) & (block == (t >> 5))
    picked = jnp.where(hit, 1.0, 0.0).astype(BF)
    weighted = jnp.where(hit, gate, 0.0).astype(BF)
    step = 512
    for j in range(0, d, step):
        xs = jnp.concatenate([b[:, j : j + step] for b in blocks], axis=0)
        ys = jnp.concatenate([b[:, d + j : d + j + step] for b in blocks], axis=0)
        rx = dot(picked, xs, ((1,), (0,)))
        rs = dot(weighted, ys, ((1,), (0,)))
        for o in range(N_OFF):
            part = slice(o * ROWS_W, (o + 1) * ROWS_W)
            outs[o][:, j : j + step] = jnp.concatenate([rx[part], rs[part]], axis=0).astype(BF)


def select_rows(place, blocks):
    d = (blocks[0].shape[1] - EXT) // 2
    return pl.pallas_call(
        select_kernel,
        out_shape=[jax.ShapeDtypeStruct((2 * ROWS_W, d), BF)] * N_OFF,
        in_specs=[SMEM_SPEC] + [VMEM_SPEC] * WAVE,
        out_specs=[VMEM_SPEC] * N_OFF,
        compiler_params=pltpu.CompilerParams(vmem_limit_bytes=12 * MIB),
        cost_estimate=cost(2 * 192 * 128 * 4096, 3 * MIB),
        name="select_rows",
    )(place, *blocks)


def main_kernel(me, *refs):
    wave1, wave2 = refs[:N_OFF], refs[N_OFF : 2 * N_OFF]
    wg_hbm, wu_hbm, wd_hbm = refs[2 * N_OFF : 2 * N_OFF + 3]
    x_ref, s_ref, h_ref, ga_ref, gu_ref, ext_ref = refs[2 * N_OFF + 3 : 2 * N_OFF + 9]
    wg, wu, wd, sems = refs[2 * N_OFF + 9 :]
    copies = []
    for i, (src, dst) in enumerate(((wg_hbm, wg), (wu_hbm, wu), (wd_hbm, wd))):
        copies.append(pltpu.make_async_copy(src, dst, sems.at[i]))
        copies[-1].start()
    d = x_ref.shape[1]
    per = 2 * ROWS_W
    step = 1024
    for o in range(N_OFF):
        for j in range(0, d, step):
            one = wave1[o][:, j : j + step].astype(F32)
            two = wave2[o][:, j : j + step].astype(F32)
            x_ref[o * per : (o + 1) * per, j : j + step] = jnp.concatenate(
                [one[:ROWS_W], two[:ROWS_W]], axis=0
            ).astype(BF)
            s_ref[o * per : (o + 1) * per, j : j + step] = jnp.concatenate(
                [one[ROWS_W:], two[ROWS_W:]], axis=0
            ).astype(BF)
    for copy in copies:
        copy.wait()
    rows = x_ref.shape[0]
    ff = wg.shape[1]
    x, s = x_ref[...], s_ref[...]
    total = jnp.zeros((rows, 1), F32)
    width = 256
    for j in range(0, ff, width):
        a = dot(x, wg[:, j : j + width], ((1,), (0,)))
        u = dot(x, wu[:, j : j + width], ((1,), (0,)))
        gh = dot(s, wd[j : j + width, :], ((1,), (1,)))
        sig = jax.nn.sigmoid(a)
        swish = a * sig
        hidden = (swish * u).astype(BF)
        h_ref[:, j : j + width] = hidden
        ga_ref[:, j : j + width] = (gh * u * sig * (1.0 + a * (1.0 - sig))).astype(BF)
        gu_ref[:, j : j + width] = (gh * swish).astype(BF)
        total += jnp.sum(gh * hidden.astype(F32), axis=1, keepdims=True)
    col = lax.broadcasted_iota(I32, (rows, EXT), 1)
    ext_ref[...] = jnp.where(col == me[0], total, 0.0).astype(BF)


def main_rows(me, wave1, wave2, wg, wu, wd):
    d, ff = wg.shape
    rows = EXPERTS * CAP
    any_spec = pl.BlockSpec(memory_space=pl.ANY)
    return pl.pallas_call(
        main_kernel,
        out_shape=[
            jax.ShapeDtypeStruct((rows, d), BF),
            jax.ShapeDtypeStruct((rows, d), BF),
            jax.ShapeDtypeStruct((rows, ff), BF),
            jax.ShapeDtypeStruct((rows, ff), BF),
            jax.ShapeDtypeStruct((rows, ff), BF),
            jax.ShapeDtypeStruct((rows, EXT), BF),
        ],
        in_specs=[SMEM_SPEC] + [VMEM_SPEC] * (2 * N_OFF) + [any_spec] * 3,
        out_specs=[VMEM_SPEC] * 6,
        scratch_shapes=[
            pltpu.VMEM((d, ff), BF),
            pltpu.VMEM((d, ff), BF),
            pltpu.VMEM((ff, d), BF),
            pltpu.SemaphoreType.DMA((3,)),
        ],
        compiler_params=pltpu.CompilerParams(vmem_limit_bytes=36 * MIB),
        cost_estimate=cost(6 * rows * d * ff, 16 * MIB),
        name="main_rows",
    )(me, *wave1, *wave2, wg, wu, wd)


def row_grad_kernel(ga_ref, gu_ref, ext_ref, wg_ref, wu_ref, *outs):
    j = pl.program_id(0)
    step = wg_ref.shape[0]
    per = 2 * ROWS_W
    part = dot(ga_ref[...], wg_ref[...], ((1,), (1,))) + dot(gu_ref[...], wu_ref[...], ((1,), (1,)))
    part = part.astype(BF)
    start = pl.multiple_of(j * step, step)
    d = outs[0].shape[1] - EXT
    for o in range(N_OFF):
        outs[o][:, pl.ds(start, step)] = part[o * per : (o + 1) * per]

    @pl.when(j == 0)
    def _():
        for o in range(N_OFF):
            outs[o][:, d:] = ext_ref[o * per : (o + 1) * per, :]


def row_grads(ga, gu, ext, wg, wu):
    d, ff = wg.shape
    rows = ga.shape[0]
    step = 512
    whole = lambda shape: pl.BlockSpec(shape, lambda j: (0, 0))
    return pl.pallas_call(
        row_grad_kernel,
        grid=(d // step,),
        out_shape=[jax.ShapeDtypeStruct((2 * ROWS_W, d + EXT), BF)] * N_OFF,
        in_specs=[whole((rows, ff)), whole((rows, ff)), whole((rows, EXT))]
        + [pl.BlockSpec((step, ff), lambda j: (j, 0))] * 2,
        out_specs=[whole((2 * ROWS_W, d + EXT))] * N_OFF,
        compiler_params=pltpu.CompilerParams(vmem_limit_bytes=24 * MIB),
        cost_estimate=cost(4 * rows * d * ff, 10 * MIB),
        name="row_grads",
    )(ga, gu, ext, wg, wu)


def return_kernel(place, *refs):
    backs, blocks = refs[:N_OFF], refs[N_OFF : N_OFF + NZ]
    out_ref, table = refs[N_OFF + NZ :]
    xi, zi, ci = place[0], place[1], place[2]
    tok = blocks[0].shape[0]
    for q in range(NZ):
        table[q * tok : (q + 1) * tok, :] = blocks[q][...]
    rows = EXPERTS * CAP
    per = 2 * ROWS_W
    r = lax.broadcasted_iota(I32, (rows, EXT), 0)
    col = lax.broadcasted_iota(I32, (rows, EXT), 1)
    expert = expert_of((r * 1366) >> 16, xi, zi, ci)
    pick = (col == expert).astype(F32).astype(BF)
    r = lax.broadcasted_iota(I32, (tok, rows), 1)
    m = r - ((r * 1366) >> 16) * per
    block = (m * 10923) >> 16
    want = (m - block * CAP + 1).astype(F32)
    hits = []
    for s in range(NZ):
        rel = (s - zi) & (NZ - 1)
        q = jnp.where(rel <= NZ // 2, jnp.maximum(2 * rel - 1, 0), 2 * (NZ - rel))
        ext = table[pl.ds(pl.multiple_of(q * tok, tok), tok), :]
        code = dot(ext, pick, ((1,), (1,)))
        hits.append(jnp.where((code == want) & (block == q), 1.0, 0.0))
    hits = jnp.concatenate(hits, axis=0).astype(BF)
    width = out_ref.shape[2]
    step = 640
    for j in range(0, width, step):
        n = min(step, width - j)
        rows_j = jnp.concatenate([b[:, j : j + n] for b in backs], axis=0)
        out_ref[:, :, j : j + n] = dot(hits, rows_j, ((1,), (0,))).astype(BF).reshape(NZ, tok, n)


def return_rows(place, backs, blocks):
    tok = blocks[0].shape[0]
    width = backs[0].shape[1]
    d2 = blocks[0].shape[1] - EXT
    block_spec = pl.BlockSpec((tok, EXT), lambda i: (0, d2 // EXT))
    whole = pl.BlockSpec(backs[0].shape, lambda i: (0, 0))
    return pl.pallas_call(
        return_kernel,
        grid=(1,),
        out_shape=jax.ShapeDtypeStruct((NZ, tok, width), BF),
        in_specs=[SMEM_SPEC] + [whole] * N_OFF + [block_spec] * NZ,
        out_specs=pl.BlockSpec((NZ, tok, width), lambda i: (0, 0, 0)),
        scratch_shapes=[pltpu.VMEM((NZ * tok, EXT), BF)],
        compiler_params=pltpu.CompilerParams(vmem_limit_bytes=20 * MIB),
        cost_estimate=cost(2 * 256 * 384 * width, 3 * MIB),
        name="return_rows",
    )(place, *backs, *blocks)


def z_shift(v, by):
    return lax.ppermute(v, "z", [(i, (i + by) % NZ) for i in range(NZ)])


def xc_shift(v, dx, dc):
    return lax.ppermute(
        v, ("x", "c"), [(x * 2 + c, ((x + dx) % NX) * 2 + (c ^ dc)) for x in range(NX) for c in (0, 1)]
    )


def swap(v, order):
    pairs = [(0, 1), (1, 0), (2, 3), (3, 2)] if order == 1 else [(0, 3), (3, 0), (1, 2), (2, 1)]
    return lax.ppermute(v, "dp", pairs)


def exchange(parts, sign):
    return [parts[0]] + [xc_shift(p, sign * dx, dc) for p, (dx, dc) in zip(parts[1:], OFFSETS[1:])]


def per_device(tokens, grad_out, expert_ids, gate_values, w_gate, w_up, w_down):
    tok_dev, features = tokens.shape
    hidden_units = w_gate.shape[2]
    g, xi, zi, ci = (lax.axis_index(name) for name in AXES)
    place = jnp.stack([xi, zi, ci]).astype(I32)
    me = (xi * (2 * NZ) + zi * 2 + ci).astype(I32).reshape(1)
    wg, wu, wd = w_gate[0], w_up[0], w_down[0]

    named = expert_ids[:, :, None] == jnp.arange(EXPERTS, dtype=I32)[None, None, :]
    chosen = jnp.any(named, axis=1)
    before = (jnp.arange(tok_dev)[:, None] > jnp.arange(tok_dev)[None, :]).astype(BF)
    slot = dot(before, chosen.astype(BF), ((1,), (0,)))
    code = jnp.where(chosen, slot + 1.0, 0.0).astype(BF)
    gate_of = jnp.sum(jnp.where(named, gate_values[:, :, None].astype(F32), 0.0), axis=1).astype(BF)
    own = jnp.concatenate([tokens, grad_out, code, gate_of], axis=1)

    half = own.shape[1] // 256 * 128
    l1, r1 = z_shift(own, -1), z_shift(own, 1)
    l2, r2 = z_shift(l1, -1), z_shift(r1, 1)
    l3, r3 = z_shift(l2, -1), z_shift(r2, 1)
    far = jnp.concatenate([z_shift(l3[:, :half], -1), z_shift(r3[:, half:], 1)], axis=1)
    blocks = [own, l1, r1, l2, r2, l3, r3, far]
    wave1 = exchange(select_rows(place, blocks[:WAVE]), 1)
    wave2 = exchange(select_rows(place, blocks[WAVE:]), 1)
    x_rows, scaled, hidden, ga, gu, ext = main_rows(me, wave1, wave2, wg, wu, wd)

    dq = features // 4
    fq = hidden_units // 4
    hd = features // 2
    s_left, s_right = scaled[:, :hd], scaled[:, hd:]

    def x_part(q, ct):
        return dot(lax.dynamic_slice_in_dim(x_rows, q * dq, dq, 1), ct, ((0,), (0,)))

    def h_part(q, s):
        return dot(lax.dynamic_slice_in_dim(hidden, q * fq, fq, 1), s, ((0,), (0,)))

    streams = [(x_part, ga, 1, 3), (x_part, gu, 3, 1), (h_part, s_left, 1, 3), (h_part, s_right, 3, 1)]
    far_sent = [f(g ^ 2, v).astype(BF) for f, v, _, _ in streams]
    near_sent = [f(g ^ p, v).astype(BF) for f, v, p, _ in streams]
    far_got = [swap(v, p) for v, (_, _, p, _) in zip(far_sent, streams)]
    near_got = [swap(v, p) for v, (_, _, p, _) in zip(near_sent, streams)]

    ga_b, gu_b, _ = lax.optimization_barrier((ga, gu, (far_sent, near_sent)))
    back = exchange(row_grads(ga_b, gu_b, ext, wg, wu), -1)

    second = [
        swap((f(g ^ p2, v) + got.astype(F32)).astype(BF), p2)
        for got, (f, v, _, p2) in zip(far_got, streams)
    ]
    kept = [f(g, v) + got.astype(F32) for got, (f, v, _, _) in zip(near_got, streams)]
    gate_wg, up_wg, down_l, down_r = [
        (k + got.astype(F32)).astype(BF) for k, got in zip(kept, second)
    ]
    down_wg = jnp.concatenate([down_l, down_r], axis=1)

    summed = return_rows(place, back, blocks)
    summed = lax.all_to_all(summed, "z", split_axis=0, concat_axis=0, tiled=True)
    total = jnp.sum(summed.astype(F32), axis=0)
    token_grad = total[:, :features].astype(BF)
    gate_cols = total[:, features : features + EXPERTS]
    gate_grad = jnp.sum(jnp.where(named, gate_cols[:, None, :], 0.0), axis=2)
    gate_grad = (gate_grad / gate_values.astype(F32)).astype(BF)
    return (token_grad, gate_grad, gate_wg[None], up_wg[None], down_wg[None])


def solution(mesh):
    inner = Mesh(mesh.devices.reshape(4, NX, NZ, 2), AXES)
    tok = P(AXES, None)
    weight = P(("x", "z", "c"), None, None)
    grad = P(("x", "z", "c"), "dp", None)
    return jax.shard_map(
        per_device,
        mesh=inner,
        in_specs=(tok, tok, tok, tok, weight, weight, weight),
        out_specs=(tok, tok, grad, grad, grad),
        check_vma=False,
    )
```

```python
import functools

import jax
import jax.numpy as jnp
from jax import lax
from jax.experimental import pallas as pl
from jax.experimental.pallas import tpu as pltpu
from jax.sharding import Mesh
from jax.sharding import PartitionSpec as P

BF = jnp.bfloat16
F32 = jnp.float32
I32 = jnp.int32
AXES = ("dp", "x", "z", "c")
CAP = 6
NX = 4
NZ = 8
EXPERTS = 64
EXT = 128
N_XC = 8
WAVE = 4
ROWS_W = WAVE * CAP
WAVE_ROWS = N_XC * ROWS_W
MIB = 1 << 20
SMEM_SPEC = pl.BlockSpec(memory_space=pltpu.SMEM)
ANY_SPEC = pl.BlockSpec(memory_space=pl.ANY)


def dot(a, b, dims):
    return lax.dot_general(a, b, (dims, ((), ())), preferred_element_type=F32)


def cost(flops, nbytes):
    return pl.CostEstimate(flops=flops, bytes_accessed=nbytes, transcendentals=0)


def whole(shape):
    return pl.BlockSpec(shape, lambda i: (0,) * len(shape))


def fixed(x):
    return pltpu.with_memory_space_constraint(x, pltpu.HBM)


def pick_rows(zi, ext, n_tok, transposed):
    r = lax.broadcasted_iota(I32, (WAVE_ROWS, EXT), 0)
    col = lax.broadcasted_iota(I32, (WAVE_ROWS, EXT), 1)
    dest = (r * 2731) >> 16
    expert = (dest >> 1) * (2 * NZ) + zi * 2 + (dest & 1)
    for_code = jnp.where(col == expert, 1.0, 0.0).astype(BF)
    for_gate = jnp.where(col == expert + EXPERTS, 1.0, 0.0).astype(BF)
    row_dim = 1 if transposed else 0
    shape = (n_tok, WAVE_ROWS) if transposed else (WAVE_ROWS, n_tok)
    r = lax.broadcasted_iota(I32, shape, row_dim)
    t = lax.broadcasted_iota(I32, shape, 1 - row_dim)
    m = r - ((r * 2731) >> 16) * ROWS_W
    block = (m * 10923) >> 16
    want = (m - block * CAP + 1).astype(F32)
    if transposed:
        code = dot(ext, for_code, ((1,), (1,)))
        return (code == want) & (block == (t >> 5)), None
    code = dot(for_code, ext, ((1,), (1,)))
    gate = dot(for_gate, ext, ((1,), (1,)))
    return (code == want) & (block == (t >> 5)), gate


def select_kernel(place, b0, b1, b2, b3, out):
    blocks = (b0, b1, b2, b3)
    d = out.shape[2]
    ext = jnp.concatenate([b[:, 2 * d :] for b in blocks], axis=0)
    hit, gate = pick_rows(place[1], ext, ext.shape[0], False)
    picked = jnp.where(hit, 1.0, 0.0).astype(BF)
    weighted = jnp.where(hit, gate, 0.0).astype(BF)
    step = 512
    for j in range(0, d, step):
        xs = jnp.concatenate([b[:, j : j + step] for b in blocks], axis=0)
        ys = jnp.concatenate([b[:, d + j : d + j + step] for b in blocks], axis=0)
        rx = dot(picked, xs, ((1,), (0,)))
        rs = dot(weighted, ys, ((1,), (0,)))
        for o in range(N_XC):
            part = slice(o * ROWS_W, (o + 1) * ROWS_W)
            out[o, :, j : j + step] = jnp.concatenate([rx[part], rs[part]], axis=0).astype(BF)


def select_rows(place, blocks):
    d = (blocks[0].shape[1] - EXT) // 2
    shape = (N_XC, 2 * ROWS_W, d)
    return pl.pallas_call(
        select_kernel,
        grid=(1,),
        out_shape=pltpu.HBM(shape, BF),
        in_specs=[SMEM_SPEC] + [whole(blocks[0].shape)] * WAVE,
        out_specs=whole(shape),
        compiler_params=pltpu.CompilerParams(vmem_limit_bytes=16 * MIB),
        cost_estimate=cost(2 * 192 * 128 * 4096, 3 * MIB),
        name="select_rows",
    )(place, *[fixed(b) for b in blocks])


def main_kernel(place, got_hbm, wg_hbm, wu_hbm, wd_hbm, *refs):
    q0, q1, q3, q2, s_ref, h_ref, g_ref, back_ref = refs[:8]
    got, wg, wu, wd, x_ref, sems = refs[8:]
    copies = []
    for i, (src, dst) in enumerate(((got_hbm, got), (wg_hbm, wg), (wu_hbm, wu), (wd_hbm, wd))):
        copies.append(pltpu.make_async_copy(src, dst, sems.at[i]))
        copies[-1].start()
    copies[0].wait()
    d, ff = wg.shape
    step = 512
    for o in range(0, N_XC, 2):
        for j in range(0, d, step):
            one = got[o, :, j : j + step].astype(F32)
            two = got[o + 1, :, j : j + step].astype(F32)
            rows = slice(o * ROWS_W, (o + 2) * ROWS_W)
            x_ref[rows, j : j + step] = jnp.concatenate([one[:ROWS_W], two[:ROWS_W]], axis=0).astype(BF)
            s_ref[rows, j : j + step] = jnp.concatenate([one[ROWS_W:], two[ROWS_W:]], axis=0).astype(BF)
    dq = q0.shape[1]
    dp = place[3]
    for by, ref in ((0, q0), (1, q1), (3, q3), (2, q2)):
        ref[...] = x_ref[:, pl.ds(pl.multiple_of((dp ^ by) * dq, dq), dq)]
    x = x_ref[...]
    copies[1].wait()
    a = dot(x, wg[...], ((1,), (0,)))
    copies[2].wait()
    u = dot(x, wu[...], ((1,), (0,)))
    copies[3].wait()
    gh = dot(s_ref[...], wd[...], ((1,), (1,)))
    sig = jax.nn.sigmoid(a)
    swish = a * sig
    hidden = (swish * u).astype(BF)
    h_ref[...] = hidden
    ga = (gh * u * sig * (1.0 + a * (1.0 - sig))).astype(BF)
    gu = (gh * swish).astype(BF)
    g_ref[:, :ff] = ga
    g_ref[:, ff:] = gu
    total = jnp.sum(gh * hidden.astype(F32), axis=1, keepdims=True)
    for j in range(0, d, step):
        part = dot(ga, wg[j : j + step, :], ((1,), (1,))) + dot(gu, wu[j : j + step, :], ((1,), (1,)))
        for o in range(N_XC):
            back_ref[o, :, j : j + step] = part[o * ROWS_W : (o + 1) * ROWS_W].astype(BF)
    col = lax.broadcasted_iota(I32, (WAVE_ROWS, EXT), 1)
    me = place[0] * (2 * NZ) + place[1] * 2 + place[2]
    ext = jnp.where(col == me, total, 0.0)
    for o in range(N_XC):
        back_ref[o, :, d:] = ext[o * ROWS_W : (o + 1) * ROWS_W].astype(BF)


def main_rows(place, got, wg, wu, wd):
    d, ff = wg.shape
    rows = WAVE_ROWS
    shapes = [(rows, d // 4)] * 4 + [(rows, d), (rows, ff), (rows, 2 * ff), (N_XC, ROWS_W, d + EXT)]
    return pl.pallas_call(
        main_kernel,
        grid=(1,),
        out_shape=[pltpu.HBM(s, BF) for s in shapes],
        in_specs=[SMEM_SPEC] + [ANY_SPEC] * 4,
        out_specs=[whole(s) for s in shapes],
        scratch_shapes=[
            pltpu.VMEM(got.shape, BF),
            pltpu.VMEM((d, ff), BF),
            pltpu.VMEM((d, ff), BF),
            pltpu.VMEM((ff, d), BF),
            pltpu.VMEM((rows, d), BF),
            pltpu.SemaphoreType.DMA((4,)),
        ],
        compiler_params=pltpu.CompilerParams(vmem_limit_bytes=40 * MIB),
        cost_estimate=cost(10 * rows * d * ff, 16 * MIB),
        name="main_rows",
    )(place, *[fixed(v) for v in (got, wg, wu, wd)])


def down_kernel(h1, h2, s1, s2, out):
    out[...] = (dot(h1[...], s1[...], ((0,), (0,))) + dot(h2[...], s2[...], ((0,), (0,)))).astype(BF)


def down_partial(h, s):
    rows, ff = h[0].shape
    d = s[0].shape[1]
    step = 512
    return pl.pallas_call(
        down_kernel,
        grid=(d // step,),
        out_shape=pltpu.HBM((ff, d), BF),
        in_specs=[whole((rows, ff))] * 2 + [pl.BlockSpec((rows, step), lambda j: (0, j))] * 2,
        out_specs=pl.BlockSpec((ff, step), lambda j: (0, j)),
        compiler_params=pltpu.CompilerParams(vmem_limit_bytes=24 * MIB),
        cost_estimate=cost(4 * rows * d * ff, 5 * MIB),
        name="down_partial",
    )(*[fixed(v) for v in (*h, *s)])


def quarter_first_kernel(n, *refs):
    acc = refs[-1]
    ins = refs[:-1]
    total = None
    for x, g in zip(ins[:n], ins[n:]):
        part = dot(x[...], g[...], ((0,), (0,)))
        total = part if total is None else total + part
    acc[...] = total


def quarter_last_kernel(n, *refs):
    acc, gate, up = refs[-3:]
    ins = refs[:-3]
    ff = gate.shape[1]
    total = acc[...]
    for x, g in zip(ins[:n], ins[n:]):
        total = total + dot(x[...], g[...], ((0,), (0,)))
    gate[...] = total[:, :ff].astype(BF)
    up[...] = total[:, ff:].astype(BF)


def quarter_sums(xs, gs, acc=None):
    dq = xs[0].shape[1]
    width = gs[0].shape[1]
    n = len(xs)
    ins = [fixed(v) for v in (*xs, *gs)]
    specs = [whole(v.shape) for v in (*xs, *gs)]
    rows = sum(v.shape[0] for v in xs)
    args = dict(
        grid=(1,),
        compiler_params=pltpu.CompilerParams(vmem_limit_bytes=40 * MIB),
        cost_estimate=cost(2 * rows * dq * width, 8 * MIB),
    )
    if acc is None:
        return pl.pallas_call(
            functools.partial(quarter_first_kernel, n),
            out_shape=pltpu.HBM((dq, width), F32),
            in_specs=specs,
            out_specs=whole((dq, width)),
            name="quarter_first",
            **args,
        )(*ins)
    out = (dq, width // 2)
    return pl.pallas_call(
        functools.partial(quarter_last_kernel, n),
        out_shape=[pltpu.HBM(out, BF)] * 2,
        in_specs=specs + [whole((dq, width))],
        out_specs=[whole(out)] * 2,
        name="quarter_last",
        **args,
    )(*ins, fixed(acc))


def return_kernel(place, back, e0, e1, e2, e3, *outs):
    ext = jnp.concatenate([e[...] for e in (e0, e1, e2, e3)], axis=0)
    tok = outs[0].shape[0]
    hit, _ = pick_rows(place[1], ext, WAVE * tok, True)
    hit = jnp.where(hit, 1.0, 0.0).astype(BF)
    width = outs[0].shape[1]
    step = 640
    for j in range(0, width, step):
        n = min(step, width - j)
        rows = jnp.concatenate([back[o, :, j : j + n].astype(F32) for o in range(N_XC)], axis=0)
        part = dot(hit, rows.astype(BF), ((1,), (0,))).astype(BF)
        for b in range(WAVE):
            outs[b][:, j : j + n] = part[b * tok : (b + 1) * tok]


def return_rows(place, back, blocks):
    tok = blocks[0].shape[0]
    width = back.shape[2]
    at = (blocks[0].shape[1] - EXT) // EXT
    return pl.pallas_call(
        return_kernel,
        grid=(1,),
        out_shape=[pltpu.HBM((tok, width), BF)] * WAVE,
        in_specs=[SMEM_SPEC, whole(back.shape)] + [pl.BlockSpec((tok, EXT), lambda i: (0, at))] * WAVE,
        out_specs=[whole((tok, width))] * WAVE,
        compiler_params=pltpu.CompilerParams(vmem_limit_bytes=16 * MIB),
        cost_estimate=cost(2 * 128 * 192 * width, 2 * MIB),
        name="return_rows",
    )(place, *[fixed(v) for v in (back, *blocks)])


def z_shift(v, by):
    return lax.ppermute(v, "z", [(i, (i + by) % NZ) for i in range(NZ)])


def swap(v, by):
    return lax.ppermute(v, "dp", [(i, i ^ by) for i in range(4)])


def exchange(v):
    return lax.all_to_all(v, ("x", "c"), split_axis=0, concat_axis=0, tiled=True)


def gather_dp(v):
    mid = v.shape[0] // 2
    one, three = swap(v, 1), swap(v, 3)
    return one, three, swap(one[:mid], 3), swap(three[mid:], 1)


def per_device(tokens, grad_out, expert_ids, gate_values, w_gate, w_up, w_down):
    tok_dev, features = tokens.shape
    place = jnp.stack([lax.axis_index(name) for name in ("x", "z", "c", "dp")]).astype(I32)
    wg, wu, wd = w_gate[0], w_up[0], w_down[0]

    named = expert_ids[:, :, None] == jnp.arange(EXPERTS, dtype=I32)[None, None, :]
    chosen = jnp.any(named, axis=1)
    before = (jnp.arange(tok_dev)[:, None] > jnp.arange(tok_dev)[None, :]).astype(BF)
    slot = dot(before, chosen.astype(BF), ((1,), (0,)))
    code = jnp.where(chosen, slot + 1.0, 0.0).astype(BF)
    gate_of = jnp.sum(jnp.where(named, gate_values[:, :, None].astype(F32), 0.0), axis=1).astype(BF)
    own = jnp.concatenate([tokens, grad_out, code, gate_of], axis=1)

    half = own.shape[1] // 256 * 128
    l1, r1 = z_shift(own, -1), z_shift(own, 1)
    l2, r2 = z_shift(l1, -1), z_shift(r1, 1)
    first = [own, l1, r1, l2]
    got1 = exchange(select_rows(place, first))
    l3, r3 = z_shift(l2, -1), z_shift(r2, 1)
    far = jnp.concatenate([z_shift(l3[:, :half], -1), z_shift(r3[:, half:], 1)], axis=1)
    last = [r2, l3, r3, far]
    got2 = exchange(select_rows(place, last))

    waves = []
    for got in (got1, got2):
        q0, q1, q3, q2, s, h, g, back = main_rows(place, got, wg, wu, wd)
        cols = [q0, swap(q1, 1), swap(q3, 3), swap(q2, 2)]
        waves.append((cols, s, h, g, gather_dp(g), exchange(back)))
    (cols1, s1, h1, g1, all1, back1), (cols2, s2, h2, g2, all2, back2) = waves

    down = down_partial((h1, h2), (s1, s2))
    down_wg = lax.psum_scatter(down, "dp", scatter_dimension=0, tiled=True)

    mid = g1.shape[0] // 2
    one, three, two_a, two_b = all1
    acc = quarter_sums(
        [cols1[0], cols1[1], cols1[2], cols1[3][:mid], cols1[3][mid:], cols2[0]],
        [g1, one, three, two_a, two_b, g2],
    )
    one, three, two_a, two_b = all2
    gate_wg, up_wg = quarter_sums(
        [cols2[1], cols2[2], cols2[3][:mid], cols2[3][mid:]], [one, three, two_a, two_b], acc
    )

    home = []
    for back, blocks, steps in ((back1, first, (0, 1, -1, 2)), (back2, last, (-2, 3, -3, 4))):
        for part, by in zip(return_rows(place, back, blocks), steps):
            home.append(z_shift(part, by) if by else part)
    total = sum(v.astype(F32) for v in home)
    token_grad = total[:, :features].astype(BF)
    gate_cols = total[:, features : features + EXPERTS]
    gate_grad = jnp.sum(jnp.where(named, gate_cols[:, None, :], 0.0), axis=2)
    gate_grad = (gate_grad / gate_values.astype(F32)).astype(BF)
    return (token_grad, gate_grad, gate_wg[None], up_wg[None], down_wg[None])


def solution(mesh):
    inner = Mesh(mesh.devices.reshape(4, NX, NZ, 2), AXES)
    tok = P(AXES, None)
    weight = P(("x", "z", "c"), None, None)
    grad = P(("x", "z", "c"), "dp", None)
    return jax.shard_map(
        per_device,
        mesh=inner,
        in_specs=(tok, tok, tok, tok, weight, weight, weight),
        out_specs=(tok, tok, grad, grad, grad),
        check_vma=False,
    )
```

```python
import functools

import jax
import jax.numpy as jnp
from jax import lax
from jax.experimental import pallas as pl
from jax.experimental.pallas import tpu as pltpu
from jax.sharding import Mesh
from jax.sharding import PartitionSpec as P

BF = jnp.bfloat16
F32 = jnp.float32
I32 = jnp.int32
AXES = ("dp", "x", "z", "c")
CAP = 6
NX = 4
NZ = 8
EXPERTS = 64
EXT = 128
N_XC = 8
DEST_ROWS = NZ * CAP
ROWS = N_XC * DEST_ROWS
MIB = 1 << 20
SMEM_SPEC = pl.BlockSpec(memory_space=pltpu.SMEM)


def dot(a, b, dims):
    return lax.dot_general(a, b, (dims, ((), ())), preferred_element_type=F32)


def cost(flops, nbytes):
    return pl.CostEstimate(flops=flops, bytes_accessed=nbytes, transcendentals=0)


def whole(shape):
    return pl.BlockSpec(shape, lambda i: (0,) * len(shape))


def params(mib):
    return pltpu.CompilerParams(vmem_limit_bytes=mib * MIB)


def eye(n):
    r = lax.broadcasted_iota(I32, (n, n), 0)
    return jnp.where(r == lax.broadcasted_iota(I32, (n, n), 1), 1.0, 0.0).astype(BF)


def table_kernel(ids, gates, tokens, out):
    tok, d = tokens.shape
    shape = (EXPERTS, tok)
    e = lax.broadcasted_iota(I32, shape, 0)
    chosen = jnp.zeros(shape, F32)
    gate = jnp.zeros(shape, F32)
    for k in range(ids.shape[0]):
        named = jnp.broadcast_to(ids[k : k + 1, :], shape) == e
        chosen = jnp.where(named, 1.0, chosen)
        gate = jnp.where(named, jnp.broadcast_to(gates[k : k + 1, :].astype(F32), shape), gate)
    r = lax.broadcasted_iota(I32, (tok, tok), 0)
    earlier = jnp.where(r < lax.broadcasted_iota(I32, (tok, tok), 1), 1.0, 0.0).astype(BF)
    slot = dot(chosen.astype(BF), earlier, ((1,), (0,)))
    code = jnp.where(chosen > 0.0, slot + 1.0, 0.0)
    both = jnp.concatenate([code, gate], axis=0).astype(BF)
    out[:, :d] = tokens[...]
    out[:, d:] = dot(eye(tok), both, ((1,), (1,))).astype(BF)


def with_table(ids, gates, tokens):
    shape = (tokens.shape[0], tokens.shape[1] + EXT)
    return pl.pallas_call(
        table_kernel,
        grid=(1,),
        out_shape=jax.ShapeDtypeStruct(shape, BF),
        in_specs=[whole(ids.shape), whole(gates.shape), whole(tokens.shape)],
        out_specs=whole(shape),
        cost_estimate=cost(1 << 20, 300000),
        name="with_table",
    )(ids, gates, tokens)


def row_parts(shape, dim):
    r = lax.broadcasted_iota(I32, shape, dim)
    dest = (r * 1366) >> 16
    m = r - dest * DEST_ROWS
    block = (m * 10923) >> 16
    return dest, block, (m - block * CAP + 1).astype(F32)


def expert_columns(zi):
    dest, _, _ = row_parts((ROWS, EXT), 0)
    col = lax.broadcasted_iota(I32, (ROWS, EXT), 1)
    return col, (dest >> 1) * (2 * NZ) + zi * 2 + (dest & 1)


def select_kernel(n_ext, place, *refs):
    ext_refs, blocks = refs[:n_ext], refs[n_ext : n_ext + NZ + 1]
    out, column = refs[n_ext + NZ + 1 :]
    d = out.shape[1]
    tok = blocks[0].shape[0]
    for q in range(NZ - 1):
        column[q * tok : (q + 1) * tok, :] = blocks[q][...]
    last = slice((NZ - 1) * tok, NZ * tok)
    cut = blocks[NZ - 1].shape[1]
    column[last, :cut] = blocks[NZ - 1][...]
    column[last, cut:] = blocks[NZ][...]
    if n_ext:
        ext = jnp.concatenate([e[...] for e in ext_refs], axis=0)
    else:
        ext = column[:, d:]
    col, expert = expert_columns(place[1])
    code = dot(jnp.where(col == expert, 1.0, 0.0).astype(BF), ext, ((1,), (1,)))
    _, block, want = row_parts((ROWS, NZ * tok), 0)
    t = lax.broadcasted_iota(I32, (ROWS, NZ * tok), 1)
    hit = (code == want) & (block == (t >> 5))
    if n_ext:
        gate = dot(jnp.where(col == expert + EXPERTS, 1.0, 0.0).astype(BF), ext, ((1,), (1,)))
        pick = jnp.where(hit, gate, 0.0).astype(BF)
    else:
        pick = jnp.where(hit, 1.0, 0.0).astype(BF)
    step = 512
    for j in range(0, d, step):
        out[:, j : j + step] = dot(pick, column[:, j : j + step], ((1,), (0,))).astype(BF)


def select_rows(place, blocks, d, ext=None):
    tok, width = blocks[0].shape
    n_ext = 0 if ext is None else NZ
    at = d // EXT
    ext_spec = pl.BlockSpec((tok, EXT), lambda i: (0, at))
    ext_specs = [ext_spec] * (NZ - 1) + [pl.BlockSpec((tok, EXT), lambda i: (0, ext[-1].shape[1] // EXT - 1))] if n_ext else []
    return pl.pallas_call(
        functools.partial(select_kernel, n_ext),
        grid=(1,),
        out_shape=pltpu.HBM((ROWS, d), BF),
        in_specs=[SMEM_SPEC] + ext_specs + [whole(b.shape) for b in blocks],
        out_specs=whole((ROWS, d)),
        scratch_shapes=[pltpu.VMEM((NZ * tok, width), BF)],
        compiler_params=params(16),
        cost_estimate=cost(2 * ROWS * 256 * d, 3 * MIB),
        name="select_scaled" if n_ext else "select_x",
    )(place, *(ext or ()), *blocks)


def row_grad_kernel(me, g_ref, h_ext, wg_ref, wu_ref, out):
    j = pl.program_id(0)
    step, ff = wg_ref.shape
    part = dot(g_ref[:, :ff], wg_ref[...], ((1,), (1,))) + dot(g_ref[:, ff:], wu_ref[...], ((1,), (1,)))
    out[:, pl.ds(pl.multiple_of(j * step, step), step)] = part.astype(BF)

    @pl.when(j == 0)
    def _():
        col = lax.broadcasted_iota(I32, (ROWS, EXT), 1)
        out[:, out.shape[1] - EXT :] = jnp.where(col == me[0], h_ext[...], 0.0).astype(BF)


def row_grads(me, g, row_gate, wg, wu):
    d, ff = wg.shape
    step = 512
    return pl.pallas_call(
        row_grad_kernel,
        grid=(d // step,),
        out_shape=pltpu.HBM((ROWS, d + EXT), BF),
        in_specs=[SMEM_SPEC, whole(g.shape), whole(row_gate.shape)]
        + [pl.BlockSpec((step, ff), lambda j: (j, 0))] * 2,
        out_specs=whole((ROWS, d + EXT)),
        compiler_params=params(24),
        cost_estimate=cost(4 * ROWS * d * ff, 10 * MIB),
        name="row_grads",
    )(me, g, row_gate, wg, wu)


def return_kernel(place, back, *refs):
    ext_refs, (out, table) = refs[:NZ], refs[NZ:]
    zi = place[1]
    tok = ext_refs[0].shape[0]
    for q in range(NZ):
        table[q * tok : (q + 1) * tok, :] = ext_refs[q][...]
    col, expert = expert_columns(zi)
    pick = jnp.where(col == expert, 1.0, 0.0).astype(BF)
    _, block, want = row_parts((tok, ROWS), 1)
    hits = []
    for s in range(NZ):
        rel = (s - zi) & (NZ - 1)
        q = jnp.where(rel <= NZ // 2, jnp.maximum(2 * rel - 1, 0), 2 * (NZ - rel))
        ext = table[pl.ds(pl.multiple_of(q * tok, tok), tok), :]
        code = dot(ext, pick, ((1,), (1,)))
        hits.append(jnp.where((code == want) & (block == q), 1.0, 0.0))
    hits = jnp.concatenate(hits, axis=0).astype(BF)
    width = out.shape[1]
    step = 640
    for j in range(0, width, step):
        n = min(step, width - j)
        out[:, j : j + n] = dot(hits, back[:, j : j + n], ((1,), (0,))).astype(BF)


def return_rows(place, back, ext, d):
    tok = ext[0].shape[0]
    width = back.shape[1]
    specs = [pl.BlockSpec((tok, EXT), lambda i: (0, d // EXT))] * (NZ - 1)
    specs.append(pl.BlockSpec((tok, EXT), lambda i: (0, ext[-1].shape[1] // EXT - 1)))
    return pl.pallas_call(
        return_kernel,
        grid=(1,),
        out_shape=pltpu.HBM((NZ * tok, width), BF),
        in_specs=[SMEM_SPEC, whole(back.shape)] + specs,
        out_specs=whole((NZ * tok, width)),
        scratch_shapes=[pltpu.VMEM((NZ * tok, EXT), BF)],
        compiler_params=params(16),
        cost_estimate=cost(2 * 256 * ROWS * width, 3 * MIB),
        name="return_rows",
    )(place, back, *ext)


def finish_kernel(ids, gates, parts, token_grad, gate_grad):
    n, tok, width = parts.shape
    d = token_grad.shape[1]
    step = 512
    for j in range(0, d, step):
        total = parts[0, :, j : j + step].astype(F32)
        for i in range(1, n):
            total += parts[i, :, j : j + step].astype(F32)
        token_grad[:, j : j + step] = total.astype(BF)
    ext = parts[0, :, d:].astype(F32)
    for i in range(1, n):
        ext += parts[i, :, d:].astype(F32)
    cols = dot(ext.astype(BF), eye(tok), ((0,), (0,)))[:EXPERTS]
    e = lax.broadcasted_iota(I32, (EXPERTS, tok), 0)
    rows = []
    for k in range(ids.shape[0]):
        named = jnp.broadcast_to(ids[k : k + 1, :], (EXPERTS, tok)) == e
        rows.append(jnp.sum(jnp.where(named, cols, 0.0), axis=0, keepdims=True))
    gate_grad[...] = (jnp.concatenate(rows, axis=0) / gates[...].astype(F32)).astype(BF)


def finish(ids, gates, parts):
    n, tok, width = parts.shape
    out = (tok, width - EXT)
    return pl.pallas_call(
        finish_kernel,
        grid=(1,),
        out_shape=[jax.ShapeDtypeStruct(out, BF), jax.ShapeDtypeStruct(ids.shape, BF)],
        in_specs=[whole(ids.shape), whole(gates.shape), whole(parts.shape)],
        out_specs=[whole(out), whole(ids.shape)],
        compiler_params=params(8),
        cost_estimate=cost(1 << 20, 2 * MIB),
        name="finish",
    )(ids, gates, parts)


def z_shift(v, by):
    return lax.ppermute(v, "z", [(i, (i + by) % NZ) for i in range(NZ)])


def z_column(own):
    half = own.shape[1] // 256 * 128
    l1, r1 = z_shift(own, -1), z_shift(own, 1)
    l2, r2 = z_shift(l1, -1), z_shift(r1, 1)
    l3, r3 = z_shift(l2, -1), z_shift(r2, 1)
    return [own, l1, r1, l2, r2, l3, r3, z_shift(l3[:, :half], -1), z_shift(r3[:, half:], 1)]


def swap(v, by):
    return lax.ppermute(v, "dp", [(i, i ^ by) for i in range(4)])


def exchange(v):
    v = v.reshape(N_XC, DEST_ROWS, v.shape[1])
    v = lax.all_to_all(v, ("x", "c"), split_axis=0, concat_axis=0, tiled=True)
    return v.reshape(ROWS, v.shape[2])


def per_device(tokens, grad_out, expert_ids, gate_values, w_gate, w_up, w_down):
    tok_dev, features = tokens.shape
    ff = w_gate.shape[2]
    place = jnp.stack([lax.axis_index(name) for name in ("x", "z", "c", "dp")]).astype(I32)
    me = (place[0] * (2 * NZ) + place[1] * 2 + place[2]).reshape(1)
    g = place[3]
    wg, wu, wd = w_gate[0], w_up[0], w_down[0]
    ids, gates = expert_ids.T, gate_values.T

    blocks = z_column(with_table(ids, gates, tokens))
    table = blocks[:7] + blocks[8:]
    sent_x = select_rows(place, blocks, features)
    sent_x, grad_out = lax.optimization_barrier((sent_x, grad_out))
    x_rows = exchange(sent_x)
    scaled = exchange(select_rows(place, z_column(grad_out), features, table))

    dq = features // 4

    def x_quarter(by):
        return lax.dynamic_slice_in_dim(x_rows, (g ^ by) * dq, dq, 1)

    x_own = x_quarter(0)
    x_one, x_three, x_two = [swap(x_quarter(by), by) for by in (1, 3, 2)]
    a = dot(x_rows, wg, ((1,), (0,)))
    u = dot(x_rows, wu, ((1,), (0,)))
    sig = jax.nn.sigmoid(a)
    swish = a * sig
    hidden = (swish * u).astype(BF)
    slope = u * sig * (1.0 + a * (1.0 - sig))
    scaled, x_one, x_three, x_two, swish, slope, hidden = lax.optimization_barrier(
        (scaled, x_one, x_three, x_two, swish, slope, hidden)
    )
    gh = dot(scaled, wd, ((1,), (1,)))
    ga = (gh * slope).astype(BF)
    gu = (gh * swish).astype(BF)
    row_gate = jnp.sum(gh * hidden.astype(F32), axis=1, keepdims=True)
    ga_gu = jnp.concatenate([ga, gu], axis=1)

    mid = ROWS // 2
    g_one, g_three = swap(ga_gu, 1), swap(ga_gu, 3)

    fq = ff // 4
    hd = features // 2
    s_left, s_right = scaled[:, :hd], scaled[:, hd:]

    def h_part(q, s):
        return dot(lax.dynamic_slice_in_dim(hidden, q * fq, fq, 1), s, ((0,), (0,)))

    streams = [(s_left, 1, 3), (s_right, 3, 1)]
    far_got = [swap(h_part(g ^ 2, v).astype(BF), p) for v, p, _ in streams]
    near_got = [swap(h_part(g ^ p, v).astype(BF), p) for v, p, _ in streams]
    g_two_a, g_two_b = swap(g_one[:mid], 3), swap(g_three[mid:], 1)
    back = exchange(row_grads(me, ga_gu, row_gate, wg, wu))
    second = [
        swap((h_part(g ^ p2, v) + got.astype(F32)).astype(BF), p2)
        for got, (v, _, p2) in zip(far_got, streams)
    ]
    kept = [h_part(g, v) + got.astype(F32) for got, (v, _, _) in zip(near_got, streams)]
    down_wg = jnp.concatenate([(k + got.astype(F32)).astype(BF) for k, got in zip(kept, second)], axis=1)

    acc = dot(x_own, ga_gu, ((0,), (0,)))
    acc = acc + dot(x_one, g_one, ((0,), (0,)))
    acc = acc + dot(x_three, g_three, ((0,), (0,)))
    acc = acc + dot(x_two[:mid], g_two_a, ((0,), (0,)))
    acc = (acc + dot(x_two[mid:], g_two_b, ((0,), (0,)))).astype(BF)
    gate_wg, up_wg = acc[:, :ff], acc[:, ff:]

    summed = return_rows(place, back, table, features).reshape(NZ, tok_dev, features + EXT)
    summed = lax.all_to_all(summed, "z", split_axis=0, concat_axis=0, tiled=True)
    token_grad, gate_grad = finish(ids, gates, summed)
    return (token_grad, gate_grad.T, gate_wg[None], up_wg[None], down_wg[None])


def solution(mesh):
    inner = Mesh(mesh.devices.reshape(4, NX, NZ, 2), AXES)
    tok = P(AXES, None)
    weight = P(("x", "z", "c"), None, None)
    grad = P(("x", "z", "c"), "dp", None)
    return jax.shard_map(
        per_device,
        mesh=inner,
        in_specs=(tok, tok, tok, tok, weight, weight, weight),
        out_specs=(tok, tok, grad, grad, grad),
        check_vma=False,
    )
```

```python
import functools

import jax
import jax.numpy as jnp
from jax import lax
from jax.experimental import pallas as pl
from jax.experimental.pallas import tpu as pltpu
from jax.sharding import Mesh
from jax.sharding import PartitionSpec as P

BF = jnp.bfloat16
F32 = jnp.float32
I32 = jnp.int32
AXES = ("dp", "x", "z", "c")
CAP = 6
NX = 4
NZ = 8
EXPERTS = 64
EXT = 128
N_XC = 8
DEST_ROWS = NZ * CAP
ROWS = N_XC * DEST_ROWS
MIB = 1 << 20
SMEM_SPEC = pl.BlockSpec(memory_space=pltpu.SMEM)


def dot(a, b, dims):
    return lax.dot_general(a, b, (dims, ((), ())), preferred_element_type=F32)


def cost(flops, nbytes):
    return pl.CostEstimate(flops=flops, bytes_accessed=nbytes, transcendentals=0)


def whole(shape):
    return pl.BlockSpec(shape, lambda i: (0,) * len(shape))


def params():
    return pltpu.CompilerParams(vmem_limit_bytes=58 * MIB)


def eye(n):
    r = lax.broadcasted_iota(I32, (n, n), 0)
    return jnp.where(r == lax.broadcasted_iota(I32, (n, n), 1), 1.0, 0.0).astype(BF)


def pack_kernel(ids, gates, tokens, grads, packed, payload):
    tok, d = tokens.shape
    wide = ids.shape[1]
    dq = d // 4
    shape = (EXPERTS, wide)
    e = lax.broadcasted_iota(I32, shape, 0)
    chosen = jnp.zeros(shape, F32)
    gate = jnp.zeros(shape, F32)
    for k in range(ids.shape[0]):
        named = jnp.broadcast_to(ids[k : k + 1, :], shape) == e
        chosen = jnp.where(named, 1.0, chosen)
        gate = jnp.where(named, jnp.broadcast_to(gates[k : k + 1, :].astype(F32), shape), gate)
    r = lax.broadcasted_iota(I32, (wide, wide), 0)
    c = lax.broadcasted_iota(I32, (wide, wide), 1)
    earlier = jnp.where((r < c) & ((r >> 5) == (c >> 5)), 1.0, 0.0).astype(BF)
    slot = dot(chosen.astype(BF), earlier, ((1,), (0,)))
    code = jnp.where(chosen > 0.0, slot + 1.0, 0.0)
    both = jnp.concatenate([code, gate], axis=0).astype(BF)
    r = lax.broadcasted_iota(I32, (tok, wide), 0)
    one = jnp.where(r == lax.broadcasted_iota(I32, (tok, wide), 1), 1.0, 0.0).astype(BF)
    payload[:, :d] = grads[...]
    payload[:, d:] = dot(one, both, ((1,), (1,))).astype(BF)

    rows = packed.shape[0]
    r = lax.broadcasted_iota(I32, (rows, EXPERTS), 0)
    own = jnp.where((r >> 3) == lax.broadcasted_iota(I32, (rows, EXPERTS), 1), 1.0, 0.0).astype(BF)
    code = dot(own, code.astype(BF), ((1,), (0,)))
    q = lax.broadcasted_iota(I32, (rows, wide), 0) & 7
    quarter = (q & 3) == (lax.broadcasted_iota(I32, (rows, wide), 1) >> 5)
    x4 = jnp.concatenate([tokens[:, k * dq : (k + 1) * dq] for k in range(4)], axis=0)
    for p in range(CAP // 2):
        want = ((q >> 2) + (2 * p + 1)).astype(F32)
        pick = jnp.where(quarter & (code == want), 1.0, 0.0).astype(BF)
        packed[:, p * dq : (p + 1) * dq] = dot(pick, x4, ((1,), (0,))).astype(BF)


def pack(ids, gates, tokens, grads):
    tok, d = tokens.shape
    shapes = [(EXPERTS * 8, CAP * d // 8), (tok, d + EXT)]
    return pl.pallas_call(
        pack_kernel,
        grid=(1,),
        out_shape=[pltpu.HBM(v, BF) for v in shapes],
        in_specs=[whole(v.shape) for v in (ids, gates, tokens, grads)],
        out_specs=[whole(v) for v in shapes],
        compiler_params=params(),
        cost_estimate=cost(1 << 28, 3 * MIB),
        name="pack",
    )(ids, gates, tokens, grads)


def row_parts(shape, dim):
    r = lax.broadcasted_iota(I32, shape, dim)
    dest = (r * 1366) >> 16
    m = r - dest * DEST_ROWS
    z = (m * 10923) >> 16
    return dest, z, m - z * CAP


def expert_columns(zi):
    dest, _, _ = row_parts((ROWS, EXT), 0)
    col = lax.broadcasted_iota(I32, (ROWS, EXT), 1)
    return col, (dest >> 1) * (2 * NZ) + zi * 2 + (dest & 1)


def select_kernel(place, *refs):
    blocks = refs[: NZ + 1]
    out, table, column = refs[NZ + 1 :]
    d = out.shape[1]
    tok = blocks[0].shape[0]
    for q in range(NZ - 1):
        column[q * tok : (q + 1) * tok, :] = blocks[q][...]
    last = slice((NZ - 1) * tok, NZ * tok)
    half = blocks[NZ - 1].shape[1]
    column[last, :half] = blocks[NZ - 1][...]
    column[last, half:] = blocks[NZ][...]
    ext = column[:, d:]
    table[...] = ext
    col, expert = expert_columns(place[1])
    code = dot(jnp.where(col == expert, 1.0, 0.0).astype(BF), ext, ((1,), (1,)))
    gate = dot(jnp.where(col == expert + EXPERTS, 1.0, 0.0).astype(BF), ext, ((1,), (1,)))
    _, z, slot = row_parts((ROWS, NZ * tok), 0)
    q = lax.broadcasted_iota(I32, (ROWS, NZ * tok), 1) >> 5
    rel = jnp.where((q & 1) == 1, (q + 1) >> 1, NZ - (q >> 1))
    hit = (code == (slot + 1).astype(F32)) & (z == ((rel + place[1]) & (NZ - 1)))
    pick = jnp.where(hit, gate, 0.0).astype(BF)
    step = 512
    for j in range(0, d, step):
        out[:, j : j + step] = dot(pick, column[:, j : j + step], ((1,), (0,))).astype(BF)


def select_scaled(place, blocks, d):
    tok, width = blocks[0].shape
    n = NZ * tok
    return pl.pallas_call(
        select_kernel,
        grid=(1,),
        out_shape=[pltpu.HBM((ROWS, d), BF), pltpu.HBM((n, EXT), BF)],
        in_specs=[SMEM_SPEC] + [whole(b.shape) for b in blocks],
        out_specs=[whole((ROWS, d)), whole((n, EXT))],
        scratch_shapes=[pltpu.VMEM((n, width), BF)],
        compiler_params=params(),
        cost_estimate=cost(2 * ROWS * n * d, 3 * MIB),
        name="select_scaled",
    )(place, *blocks)


def forward_kernel(place, got, wg, wu, q0, q1, q3, q2, slope, swish, hidden, h4, x_ref):
    rows, dq = q0.shape
    n = got.shape[0]
    dest, z, slot = row_parts((rows, n), 0)
    col = lax.broadcasted_iota(I32, (rows, n), 1)
    base = ((dest >> 1) * (2 * NZ) + z * 2 + (dest & 1)) * 8 + (slot & 1) * 4
    pair = slot >> 1
    for k in range(4):
        total = None
        for p in range(CAP // 2):
            pick = jnp.where((col == base + k) & (pair == p), 1.0, 0.0).astype(BF)
            part = dot(pick, got[:, p * dq : (p + 1) * dq], ((1,), (0,)))
            total = part if total is None else total + part
        x_ref[:, k * dq : (k + 1) * dq] = total.astype(BF)
    for by, ref in ((0, q0), (1, q1), (3, q3), (2, q2)):
        ref[...] = x_ref[:, pl.ds(pl.multiple_of((place[3] ^ by) * dq, dq), dq)]
    x = x_ref[...]
    a = dot(x, wg[...], ((1,), (0,)))
    u = dot(x, wu[...], ((1,), (0,)))
    sig = jax.nn.sigmoid(a)
    sw = a * sig
    swish[...] = sw
    slope[...] = u * sig * (1.0 + a * (1.0 - sig))
    h = (sw * u).astype(BF)
    hidden[...] = h
    fq = h4.shape[2]
    for k in range(4):
        h4[k] = h[:, k * fq : (k + 1) * fq]


def forward(place, got, wg, wu):
    d, ff = wg.shape
    shapes = [((ROWS, d // 4), BF)] * 4 + [((ROWS, ff), F32)] * 2 + [((ROWS, ff), BF), ((4, ROWS, ff // 4), BF)]
    return pl.pallas_call(
        forward_kernel,
        grid=(1,),
        out_shape=[pltpu.HBM(*v) for v in shapes],
        in_specs=[SMEM_SPEC, whole(got.shape), whole(wg.shape), whole(wu.shape)],
        out_specs=[whole(v) for v, _ in shapes],
        scratch_shapes=[pltpu.VMEM((ROWS, d), BF)],
        compiler_params=params(),
        cost_estimate=cost(4 * ROWS * d * ff, 14 * MIB),
        name="forward",
    )(place, got, wg, wu)


def backward_kernel(place, *refs):
    n_in, n_out = 8, 6
    hbm_in, hbm_out = refs[:n_in], refs[n_in : n_in + n_out]
    vmem_in = refs[n_in + n_out : 2 * n_in + n_out]
    vmem_out = refs[2 * n_in + n_out : 2 * (n_in + n_out)]
    sems_in, sems_out = refs[2 * (n_in + n_out) :]
    loads = [pltpu.make_async_copy(h, v, sems_in.at[i]) for i, (h, v) in enumerate(zip(hbm_in, vmem_in))]
    stores = [pltpu.make_async_copy(v, h, sems_out.at[i]) for i, (h, v) in enumerate(zip(hbm_out, vmem_out))]
    for load in loads:
        load.start()
    scaled, wd, slope, swish, hidden, h4, wg, wu = vmem_in
    g_ref, out = vmem_out[0], vmem_out[5]
    ff, d = wd.shape
    hd = d // 2
    loads[0].wait()
    loads[1].wait()
    gh = dot(scaled[...], wd[...], ((1,), (1,)))
    loads[2].wait()
    g_ref[:, :ff] = (gh * slope[...]).astype(BF)
    loads[3].wait()
    g_ref[:, ff:] = (gh * swish[...]).astype(BF)
    stores[0].start()
    loads[4].wait()
    total = jnp.sum(gh * hidden[...].astype(F32), axis=1, keepdims=True)
    col = lax.broadcasted_iota(I32, (ROWS, EXT), 1)
    me = place[0] * (2 * NZ) + place[1] * 2 + place[2]
    out[:, d:] = jnp.where(col == me, total, 0.0).astype(BF)
    loads[5].wait()
    for i, by in enumerate((2, 2, 1, 3)):
        cols = slice((i % 2) * hd, (i % 2 + 1) * hd)
        vmem_out[1 + i][...] = dot(h4[place[3] ^ by], scaled[:, cols], ((0,), (0,))).astype(BF)
        stores[1 + i].start()
    loads[6].wait()
    loads[7].wait()
    step = 512
    for j in range(0, d, step):
        part = dot(g_ref[:, :ff], wg[j : j + step, :], ((1,), (1,)))
        part += dot(g_ref[:, ff:], wu[j : j + step, :], ((1,), (1,)))
        out[:, j : j + step] = part.astype(BF)
    stores[5].start()
    for store in stores:
        store.wait()


def backward(place, scaled, wd, slope, swish, hidden, h4, wg, wu):
    ff, d = wd.shape
    shapes = [(ROWS, 2 * ff)] + [(ff // 4, d // 2)] * 4 + [(ROWS, d + EXT)]
    ins = (scaled, wd, slope, swish, hidden, h4, wg, wu)
    any_spec = pl.BlockSpec(memory_space=pl.ANY)
    return pl.pallas_call(
        backward_kernel,
        grid=(1,),
        out_shape=[pltpu.HBM(v, BF) for v in shapes],
        in_specs=[SMEM_SPEC] + [any_spec] * len(ins),
        out_specs=[any_spec] * len(shapes),
        scratch_shapes=[pltpu.VMEM(v.shape, v.dtype) for v in ins]
        + [pltpu.VMEM(v, BF) for v in shapes]
        + [pltpu.SemaphoreType.DMA((len(ins),)), pltpu.SemaphoreType.DMA((len(shapes),))],
        compiler_params=params(),
        cost_estimate=cost(8 * ROWS * d * ff, 19 * MIB),
        name="backward",
    )(place, *ins)


def next_kernel(place, h4, scaled, far_l, far_r, left, right):
    hd = far_l.shape[1]
    for i, (by, got, out) in enumerate(((3, far_l, left), (1, far_r, right))):
        part = dot(h4[place[3] ^ by], scaled[:, i * hd : (i + 1) * hd], ((0,), (0,)))
        out[...] = (part + got[...].astype(F32)).astype(BF)


def down_next(place, h4, scaled, far_l, far_r):
    ins = (h4, scaled, far_l, far_r)
    return pl.pallas_call(
        next_kernel,
        grid=(1,),
        out_shape=[pltpu.HBM(far_l.shape, BF)] * 2,
        in_specs=[SMEM_SPEC] + [whole(v.shape) for v in ins],
        out_specs=[whole(far_l.shape)] * 2,
        compiler_params=params(),
        cost_estimate=cost(1 << 28, 3 * MIB),
        name="down_next",
    )(place, *ins)


def own_kernel(place, h4, scaled, near_l, near_r, out):
    hd = near_l.shape[1]
    for i, got in enumerate((near_l, near_r)):
        part = dot(h4[place[3]], scaled[:, i * hd : (i + 1) * hd], ((0,), (0,)))
        out[:, i * hd : (i + 1) * hd] = part + got[...].astype(F32)


def down_own(place, h4, scaled, near_l, near_r):
    ins = (h4, scaled, near_l, near_r)
    shape = (near_l.shape[0], 2 * near_l.shape[1])
    return pl.pallas_call(
        own_kernel,
        grid=(1,),
        out_shape=pltpu.HBM(shape, F32),
        in_specs=[SMEM_SPEC] + [whole(v.shape) for v in ins],
        out_specs=whole(shape),
        compiler_params=params(),
        cost_estimate=cost(1 << 28, 3 * MIB),
        name="down_own",
    )(place, *ins)


def sum_kernel(n, *refs):
    acc = refs[-1]
    total = None
    for x, g in zip(refs[:n], refs[n : 2 * n]):
        part = dot(x[...], g[...], ((0,), (0,)))
        total = part if total is None else total + part
    acc[...] = total


def factor_sums(xs, gs):
    dq = xs[0].shape[1]
    ff = gs[0].shape[1] // 2
    rows = xs[0].shape[0]
    return pl.pallas_call(
        functools.partial(sum_kernel, len(xs)),
        grid=(2,),
        out_shape=pltpu.HBM((dq, 2 * ff), F32),
        in_specs=[pl.BlockSpec((rows, dq), lambda j: (0, 0))] * len(xs)
        + [pl.BlockSpec((rows, ff), lambda j: (0, j))] * len(gs),
        out_specs=pl.BlockSpec((dq, ff), lambda j: (0, j)),
        compiler_params=params(),
        cost_estimate=cost(4 * len(xs) * rows * dq * ff, 8 * MIB),
        name="factor_sums",
    )(*xs, *gs)


def last_kernel(x, g_a, g_b, acc, own, left, right, gate, up, down):
    j = pl.program_id(0)
    mid = g_a.shape[0]
    total = acc[...] + dot(x[:mid], g_a[...], ((0,), (0,))) + dot(x[mid:], g_b[...], ((0,), (0,)))
    total = total.astype(BF)

    @pl.when(j == 0)
    def _():
        gate[...] = total
        hd = left.shape[1]
        down[:, :hd] = (own[:, :hd] + left[...].astype(F32)).astype(BF)
        down[:, hd:] = (own[:, hd:] + right[...].astype(F32)).astype(BF)

    @pl.when(j == 1)
    def _():
        up[...] = total


def last_sums(x, g_a, g_b, acc, own, left, right):
    dq, width = acc.shape
    ff = width // 2
    mid = g_a.shape[0]
    const = lambda v: pl.BlockSpec(v, lambda j: (0, 0))
    half = lambda n: pl.BlockSpec((n, ff), lambda j: (0, j))
    return pl.pallas_call(
        last_kernel,
        grid=(2,),
        out_shape=[jax.ShapeDtypeStruct((dq, ff), BF)] * 2 + [jax.ShapeDtypeStruct(own.shape, BF)],
        in_specs=[const(x.shape), half(mid), half(mid), half(dq), const(own.shape), const(left.shape), const(right.shape)],
        out_specs=[const((dq, ff)), const((dq, ff)), const(own.shape)],
        compiler_params=params(),
        cost_estimate=cost(4 * 2 * mid * dq * ff, 8 * MIB),
        name="last_sums",
    )(x, g_a, g_b, acc, own, left, right)


def return_kernel(place, back, table, out):
    zi = place[1]
    tok = table.shape[0] // NZ
    col, expert = expert_columns(zi)
    pick = jnp.where(col == expert, 1.0, 0.0).astype(BF)
    _, z, slot = row_parts((tok, ROWS), 1)
    want = (slot + 1).astype(F32)
    hits = []
    for s in range(NZ):
        rel = (s - zi) & (NZ - 1)
        q = jnp.where(rel <= NZ // 2, jnp.maximum(2 * rel - 1, 0), 2 * (NZ - rel))
        ext = table[pl.ds(pl.multiple_of(q * tok, tok), tok), :]
        code = dot(ext, pick, ((1,), (1,)))
        hits.append(jnp.where((code == want) & (z == s), 1.0, 0.0))
    hits = jnp.concatenate(hits, axis=0).astype(BF)
    width = out.shape[1]
    step = 640
    for j in range(0, width, step):
        n = min(step, width - j)
        out[:, j : j + n] = dot(hits, back[:, j : j + n], ((1,), (0,))).astype(BF)


def return_rows(place, back, table):
    n = table.shape[0]
    width = back.shape[1]
    return pl.pallas_call(
        return_kernel,
        grid=(1,),
        out_shape=pltpu.HBM((n, width), BF),
        in_specs=[SMEM_SPEC, whole(back.shape), whole(table.shape)],
        out_specs=whole((n, width)),
        compiler_params=params(),
        cost_estimate=cost(2 * n * ROWS * width, 3 * MIB),
        name="return_rows",
    )(place, back, table)


def finish_kernel(ids, gates, parts, token_grad, gate_grad):
    n, tok, width = parts.shape
    d = token_grad.shape[1]
    step = 512
    for j in range(0, d, step):
        total = parts[0, :, j : j + step].astype(F32)
        for i in range(1, n):
            total += parts[i, :, j : j + step].astype(F32)
        token_grad[:, j : j + step] = total.astype(BF)
    ext = parts[0, :, d:].astype(F32)
    for i in range(1, n):
        ext += parts[i, :, d:].astype(F32)
    cols = dot(ext.astype(BF), eye(tok), ((0,), (0,)))[:EXPERTS]
    e = lax.broadcasted_iota(I32, (EXPERTS, tok), 0)
    rows = []
    for k in range(ids.shape[0]):
        named = jnp.broadcast_to(ids[k : k + 1, :], (EXPERTS, tok)) == e
        rows.append(jnp.sum(jnp.where(named, cols, 0.0), axis=0, keepdims=True))
    gate_grad[...] = (jnp.concatenate(rows, axis=0) / gates[...].astype(F32)).astype(BF)


def finish(ids, gates, parts):
    n, tok, width = parts.shape
    out = (tok, width - EXT)
    return pl.pallas_call(
        finish_kernel,
        grid=(1,),
        out_shape=[jax.ShapeDtypeStruct(out, BF), jax.ShapeDtypeStruct(ids.shape, BF)],
        in_specs=[whole(ids.shape), whole(gates.shape), whole(parts.shape)],
        out_specs=[whole(out), whole(ids.shape)],
        compiler_params=params(),
        cost_estimate=cost(1 << 20, 2 * MIB),
        name="finish",
    )(ids, gates, parts)


def z_shift(v, by):
    return lax.ppermute(v, "z", [(i, (i + by) % NZ) for i in range(NZ)])


def z_column(own):
    half = own.shape[1] // 256 * 128
    l1, r1 = z_shift(own, -1), z_shift(own, 1)
    l2, r2 = z_shift(l1, -1), z_shift(r1, 1)
    l3, r3 = z_shift(l2, -1), z_shift(r2, 1)
    return [own, l1, r1, l2, r2, l3, r3, z_shift(l3[:, :half], -1), z_shift(r3[:, half:], 1)]


def swap(v, by):
    return lax.ppermute(v, "dp", [(i, i ^ by) for i in range(4)])


def all_to_all(v, axes, parts):
    shape = (parts, v.shape[0] // parts, v.shape[1])
    return lax.all_to_all(v.reshape(shape), axes, split_axis=0, concat_axis=0, tiled=True)


def exchange(v, axes, parts):
    return all_to_all(v, axes, parts).reshape(v.shape)


def per_device(tokens, grad_out, expert_ids, gate_values, w_gate, w_up, w_down):
    features = tokens.shape[1]
    place = jnp.stack([lax.axis_index(name) for name in ("x", "z", "c", "dp")]).astype(I32)
    wg, wu, wd = w_gate[0], w_up[0], w_down[0]
    ids, gates = expert_ids.T, gate_values.T

    packed, payload = pack(jnp.tile(ids, (1, 4)), jnp.tile(gates, (1, 4)), tokens, grad_out)
    got_x = exchange(packed, ("x", "z", "c"), EXPERTS)
    sent_scaled, table = select_scaled(place, z_column(payload), features)
    got_x, sent_scaled = lax.optimization_barrier((got_x, sent_scaled))
    scaled = exchange(sent_scaled, ("x", "c"), N_XC)

    q0, q1, q3, q2, slope, swish, hidden, h4 = forward(place, got_x, wg, wu)
    x_one, x_three, x_two = swap(q1, 1), swap(q3, 3), swap(q2, 2)
    scaled, x_one, x_three, x_two, slope = lax.optimization_barrier((scaled, x_one, x_three, x_two, slope))

    g_own, far_l, far_r, near_l, near_r, sent_back = backward(
        place, scaled, wd, slope, swish, hidden, h4, wg, wu
    )
    g_one, g_three = swap(g_own, 1), swap(g_own, 3)
    far_l, far_r = swap(far_l, 1), swap(far_r, 3)
    near_l, near_r = swap(near_l, 1), swap(near_r, 3)
    back = exchange(sent_back, ("x", "c"), N_XC)

    g_one, g_three, far_l, far_r, back = lax.optimization_barrier((g_one, g_three, far_l, far_r, back))
    mid = ROWS // 2
    g_two_a, g_two_b = swap(g_one[:mid], 3), swap(g_three[mid:], 1)
    next_l, next_r = down_next(place, h4, scaled, far_l, far_r)
    next_l, next_r = swap(next_l, 3), swap(next_r, 1)
    acc = factor_sums((q0, x_one, x_three), (g_own, g_one, g_three))
    own = down_own(place, h4, scaled, near_l, near_r)

    summed = return_rows(place, back, table)
    parts = all_to_all(summed, "z", NZ)
    g_two_a, g_two_b, next_l, next_r, acc, own, _ = lax.optimization_barrier(
        (g_two_a, g_two_b, next_l, next_r, acc, own, summed)
    )
    gate_wg, up_wg, down_wg = last_sums(x_two, g_two_a, g_two_b, acc, own, next_l, next_r)
    token_grad, gate_grad = finish(ids, gates, parts)
    return (token_grad, gate_grad.T, gate_wg[None], up_wg[None], down_wg[None])


def solution(mesh):
    inner = Mesh(mesh.devices.reshape(4, NX, NZ, 2), AXES)
    tok = P(AXES, None)
    weight = P(("x", "z", "c"), None, None)
    grad = P(("x", "z", "c"), "dp", None)
    return jax.shard_map(
        per_device,
        mesh=inner,
        in_specs=(tok, tok, tok, tok, weight, weight, weight),
        out_specs=(tok, tok, grad, grad, grad),
        check_vma=False,
    )
```

```python
import functools

import jax
import jax.numpy as jnp
from jax import lax
from jax.experimental import pallas as pl
from jax.experimental.pallas import tpu as pltpu
from jax.sharding import PartitionSpec as P

BF = jnp.bfloat16
F32 = jnp.float32
I32 = jnp.int32
CAP = 6
PAIRS = CAP // 2
EXPERTS = 64
EXT = 128
ROWS = EXPERTS * CAP
MIB = 1 << 20
SMEM_SPEC = pl.BlockSpec(memory_space=pltpu.SMEM)


def dot(a, b, dims):
    return lax.dot_general(a, b, (dims, ((), ())), preferred_element_type=F32)


def cost(flops, nbytes):
    return pl.CostEstimate(flops=flops, bytes_accessed=nbytes, transcendentals=0)


def whole(shape):
    return pl.BlockSpec(shape, lambda i: (0,) * len(shape))


def params():
    return pltpu.CompilerParams(vmem_limit_bytes=58 * MIB)


ANY_SPEC = pl.BlockSpec(memory_space=pl.ANY)


def iota(shape, dim):
    return lax.broadcasted_iota(I32, shape, dim)


def one_hot(hit):
    return jnp.where(hit, 1.0, 0.0).astype(BF)


def router(ids, gates, wide):
    k_top, tok = ids.shape
    rep = one_hot(iota((tok, wide), 0) == (iota((tok, wide), 1) & (tok - 1)))
    named_by = dot(ids[...].astype(F32).astype(BF), rep, ((1,), (0,)))
    gate_by = dot(gates[...], rep, ((1,), (0,)))
    shape = (EXPERTS, wide)
    e = iota(shape, 0).astype(F32)
    chosen = jnp.zeros(shape, F32)
    gate = jnp.zeros(shape, F32)
    for k in range(k_top):
        named = jnp.broadcast_to(named_by[k : k + 1, :], shape) == e
        chosen = jnp.where(named, 1.0, chosen)
        gate = jnp.where(named, jnp.broadcast_to(gate_by[k : k + 1, :], shape), gate)
    r, c = iota((wide, wide), 0), iota((wide, wide), 1)
    slot = dot(chosen.astype(BF), one_hot((r < c) & ((r >> 5) == (c >> 5))), ((1,), (0,)))
    return jnp.where(chosen > 0.0, slot + 1.0, 0.0), gate


def pack_kernel(ids, gates, tokens, grads, packed):
    tok, d = tokens.shape
    dq = d // 4
    wide = 8 * tok
    code, gate = router(ids, gates, wide)
    rows = packed.shape[0]
    own = one_hot((iota((rows, EXPERTS), 0) >> 4) == iota((rows, EXPERTS), 1))
    code = dot(own, code.astype(BF), ((1,), (0,)))
    gate = dot(own, gate.astype(BF), ((1,), (0,)))
    r, c = iota((rows, wide), 0), iota((rows, wide), 1)
    fits = (((r >> 3) & 1) == (c >> 7)) & ((r & 3) == ((c >> 5) & 3))
    value = jnp.where(c < 4 * tok, 1.0, gate)
    base = (((r >> 2) & 1) + 1).astype(F32)
    parts = [v[:, k * dq : (k + 1) * dq] for v in (tokens, grads) for k in range(4)]
    source = jnp.concatenate(parts, axis=0)
    for p in range(PAIRS):
        pick = jnp.where(fits & (code == base + 2.0 * p), value, 0.0).astype(BF)
        packed[:, p * dq : (p + 1) * dq] = dot(pick, source, ((1,), (0,))).astype(BF)


def pack(ids, gates, tokens, grads):
    tok, d = tokens.shape
    shape = (EXPERTS * 16, CAP * d // 8)
    ins = (ids, gates, tokens, grads)
    return pl.pallas_call(
        pack_kernel,
        grid=(1,),
        out_shape=pltpu.HBM(shape, BF),
        in_specs=[whole(v.shape) for v in ins],
        out_specs=whole(shape),
        compiler_params=params(),
        cost_estimate=cost(1 << 30, 4 * MIB),
        name="pack",
    )(*ins)


def main_kernel(place, *refs):
    n_in, n_out = 4, 13
    hbm_in, hbm_out = refs[:n_in], refs[n_in : n_in + n_out]
    vmem_in = refs[n_in + n_out : 2 * n_in + n_out]
    vmem_out = refs[2 * n_in + n_out : 2 * (n_in + n_out)]
    sems_in, sems_out = refs[2 * (n_in + n_out) :]
    loads = [pltpu.make_async_copy(h, v, sems_in.at[i]) for i, (h, v) in enumerate(zip(hbm_in, vmem_in))]
    stores = [pltpu.make_async_copy(v, h, sems_out.at[i]) for i, (h, v) in enumerate(zip(hbm_out, vmem_out))]
    for load in loads:
        load.start()
    got, wg, wu, wd = vmem_in
    x_ref, s_ref, h4, g_ref = vmem_out[:4]
    back = vmem_out[12]
    d, ff = wg.shape
    dq, fq, hd = d // 4, ff // 4, d // 2
    o, c = iota((256, 256), 0), iota((256, 256), 1)
    i = o & 31
    unpick = one_hot(c == (i >> 1) * 16 + (o >> 7) * 8 + (i & 1) * 4 + ((o >> 5) & 3))
    loads[0].wait()
    for p in range(PAIRS):
        for b in range(4):
            part = dot(unpick, got[b * 256 : (b + 1) * 256, p * dq : (p + 1) * dq], ((1,), (0,))).astype(BF)
            rows = slice(p * 128 + b * 32, p * 128 + (b + 1) * 32)
            for k in range(4):
                x_ref[rows, k * dq : (k + 1) * dq] = part[k * 32 : (k + 1) * 32]
                s_ref[rows, k * dq : (k + 1) * dq] = part[128 + k * 32 : 128 + (k + 1) * 32]
    stores[0].start()
    stores[1].start()
    x = x_ref[...]
    loads[1].wait()
    a = dot(x, wg[...], ((1,), (0,)))
    loads[2].wait()
    u = dot(x, wu[...], ((1,), (0,)))
    loads[3].wait()
    gh = dot(s_ref[...], wd[...], ((1,), (1,)))
    sig = jax.nn.sigmoid(a)
    swish = a * sig
    hidden = (swish * u).astype(BF)
    g_ref[:, :ff] = (gh * (u * sig * (1.0 + a * (1.0 - sig)))).astype(BF)
    g_ref[:, ff:] = (gh * swish).astype(BF)
    total = jnp.sum(gh * hidden.astype(F32), axis=1, keepdims=True)
    for k in range(4):
        h4[k] = hidden[:, k * fq : (k + 1) * fq]
    stores[2].start()
    stores[3].start()
    me = place[0]
    for n, by, half in ((4, 2, 0), (5, 2, 1), (8, 1, 0), (9, 3, 1)):
        xq = x_ref[:, pl.ds(pl.multiple_of((me ^ by) * dq, dq), dq)]
        vmem_out[n][...] = dot(xq, g_ref[:, half * ff : (half + 1) * ff], ((0,), (0,))).astype(BF)
        stores[n].start()
        sq = s_ref[:, half * hd : (half + 1) * hd]
        vmem_out[n + 2][...] = dot(h4[me ^ by], sq, ((0,), (0,))).astype(BF)
        stores[n + 2].start()
    o, c = iota((128, 128), 0), iota((128, 128), 1)
    repick = one_hot(c == (o & 3) * 32 + (o >> 3) * 2 + ((o >> 2) & 1))
    for k in range(4):
        cols = slice(k * dq, (k + 1) * dq)
        part = dot(g_ref[:, :ff], wg[cols, :], ((1,), (1,))) + dot(g_ref[:, ff:], wu[cols, :], ((1,), (1,)))
        if k == 0:
            stores[0].wait()
        x_ref[:, cols] = part.astype(BF)
    for p in range(PAIRS):
        for b in range(4):
            rows = slice(p * 128 + b * 32, p * 128 + (b + 1) * 32)
            four = jnp.concatenate([x_ref[rows, k * dq : (k + 1) * dq] for k in range(4)], axis=0)
            back[b * 128 : (b + 1) * 128, p * dq : (p + 1) * dq] = dot(repick, four, ((1,), (0,))).astype(BF)
    lane = iota((128, EXT), 1)
    mixed = jnp.zeros((128, EXT), F32)
    for p in range(PAIRS):
        mixed = jnp.where(lane == p, total[p * 128 : (p + 1) * 128], mixed)
    o, c = iota((512, 128), 0), iota((512, 128), 1)
    spread = one_hot((c == (o >> 3) * 2 + ((o >> 2) & 1)) & ((o & 3) == 0))
    back[:, PAIRS * dq :] = dot(spread, mixed.astype(BF), ((1,), (0,))).astype(BF)
    stores[12].start()
    for store in stores[1:]:
        store.wait()


def main_rows(place, got, wg, wu, wd):
    d, ff = wg.shape
    up, down = (d // 4, ff), (ff // 4, d // 2)
    shapes = [(ROWS, d), (ROWS, d), (4, ROWS, ff // 4), (ROWS, 2 * ff)]
    shapes += [up, up, down, down] * 2 + [(EXPERTS * 8, CAP * d // 8 + EXT)]
    ins = (got, wg, wu, wd)
    return pl.pallas_call(
        main_kernel,
        grid=(1,),
        out_shape=[pltpu.HBM(v, BF) for v in shapes],
        in_specs=[SMEM_SPEC] + [ANY_SPEC] * len(ins),
        out_specs=[ANY_SPEC] * len(shapes),
        scratch_shapes=[pltpu.VMEM(v.shape, BF) for v in ins]
        + [pltpu.VMEM(v, BF) for v in shapes]
        + [pltpu.SemaphoreType.DMA((len(ins),)), pltpu.SemaphoreType.DMA((len(shapes),))],
        compiler_params=params(),
        cost_estimate=cost(14 * ROWS * d * ff, 28 * MIB),
        name="main_rows",
    )(place, *ins)


def next_kernel(place, x_ref, s_ref, h4, g_ref, *refs):
    got, outs, own = refs[:4], refs[4:8], refs[8:]
    me = place[0]
    dq, ff = got[0].shape
    hd = got[2].shape[1]

    def up_part(by, half):
        xq = x_ref[:, pl.ds(pl.multiple_of((me ^ by) * dq, dq), dq)]
        return dot(xq, g_ref[:, half * ff : (half + 1) * ff], ((0,), (0,)))

    def down_part(by, half):
        return dot(h4[me ^ by], s_ref[:, half * hd : (half + 1) * hd], ((0,), (0,)))

    for half, by in ((0, 3), (1, 1)):
        outs[half][...] = (up_part(by, half) + got[half][...].astype(F32)).astype(BF)
        outs[2 + half][...] = (down_part(by, half) + got[2 + half][...].astype(F32)).astype(BF)
    for half in (0, 1):
        own[half][...] = up_part(0, half)
        own[2][:, half * hd : (half + 1) * hd] = down_part(0, half)


def next_parts(place, x, s, h4, g, got):
    ins = (x, s, h4, g, *got)
    shapes = [(v.shape, BF) for v in got] + [(got[0].shape, F32)] * 2
    shapes.append(((got[2].shape[0], 2 * got[2].shape[1]), F32))
    return pl.pallas_call(
        next_kernel,
        grid=(1,),
        out_shape=[pltpu.HBM(*v) for v in shapes],
        in_specs=[SMEM_SPEC] + [whole(v.shape) for v in ins],
        out_specs=[whole(v) for v, _ in shapes],
        compiler_params=params(),
        cost_estimate=cost(3 * ROWS * x.shape[1] * h4.shape[2] * 4, 16 * MIB),
        name="next_parts",
    )(place, *ins)


def finish_kernel(ids, gates, got, token_grad, gate_grad):
    k_top, tok = ids.shape
    wide = 4 * tok
    dq = token_grad.shape[1] // 4
    n = got.shape[0]
    code, _ = router(ids, gates, wide)
    from_e = one_hot(iota((EXPERTS, n), 0) == (iota((EXPERTS, n), 1) >> 3))
    code_cols = dot(code.astype(BF), from_e, ((0,), (0,)))
    r, c = iota((wide, n), 0), iota((wide, n), 1)
    fits = (r >> 5) == (c & 3)
    base = (((c >> 2) & 1) + 1).astype(F32)
    total = None
    for p in range(PAIRS):
        pick = one_hot(fits & (code_cols == base + 2.0 * p))
        part = dot(pick, got[:, p * dq : (p + 1) * dq], ((1,), (0,)))
        total = part if total is None else total + part
    for k in range(4):
        token_grad[:, k * dq : (k + 1) * dq] = total[k * tok : (k + 1) * tok].astype(BF)

    code = code[:, :tok]
    by_slot = jnp.zeros((EXPERTS, tok), F32)
    r, c = iota((EXPERTS, n), 0), iota((EXPERTS, n), 1)
    for parity in range(2):
        at = one_hot(c == r * 8 + 4 * parity)
        values = dot(at, got[:, PAIRS * dq :], ((1,), (0,)))
        for p in range(PAIRS):
            by_slot = jnp.where(code == 2.0 * p + parity + 1.0, values[:, p : p + 1], by_slot)
    e = iota((EXPERTS, tok), 0)
    rows = []
    for k in range(k_top):
        named = jnp.broadcast_to(ids[k : k + 1, :], (EXPERTS, tok)) == e
        rows.append(jnp.sum(jnp.where(named, by_slot, 0.0), axis=0, keepdims=True))
    gate_grad[...] = (jnp.concatenate(rows, axis=0) / gates[...].astype(F32)).astype(BF)


def finish(ids, gates, got, d):
    out = (ids.shape[1], d)
    ins = (ids, gates, got)
    return pl.pallas_call(
        finish_kernel,
        grid=(1,),
        out_shape=[jax.ShapeDtypeStruct(out, BF), jax.ShapeDtypeStruct(ids.shape, BF)],
        in_specs=[whole(v.shape) for v in ins],
        out_specs=[whole(out), whole(ids.shape)],
        compiler_params=params(),
        cost_estimate=cost(1 << 28, 2 * MIB),
        name="finish",
    )(*ins)


def swap(v, by):
    return lax.ppermute(v, "dp", [(i, i ^ by) for i in range(4)])


def exchange(v):
    shape = (EXPERTS, v.shape[0] // EXPERTS, v.shape[1])
    return lax.all_to_all(v.reshape(shape), "expert", split_axis=0, concat_axis=0, tiled=True).reshape(v.shape)


def per_device(tokens, grad_out, expert_ids, gate_values, w_gate, w_up, w_down):
    place = lax.axis_index("dp").astype(I32).reshape(1)
    ids, gates = expert_ids.T, gate_values.T
    got = exchange(pack(ids, gates, tokens, grad_out))
    outs = main_rows(place, got, w_gate[0], w_up[0], w_down[0])
    x, s, h4, g = outs[:4]
    first = (1, 3, 1, 3)
    second = (3, 1, 3, 1)
    far = [swap(v, by) for v, by in zip(outs[4:8], first)]
    near = [swap(v, by) for v, by in zip(outs[8:12], first)]
    back = exchange(outs[12])
    *nexts, gate_own, up_own, down_own = next_parts(place, x, s, h4, g, far)
    nexts = [swap(v, by) for v, by in zip(nexts, second)]
    near = [v.astype(F32) for v in near]
    nexts = [v.astype(F32) for v in nexts]
    gate_wg = (gate_own + near[0] + nexts[0]).astype(BF)
    up_wg = (up_own + near[1] + nexts[1]).astype(BF)
    down_wg = down_own + jnp.concatenate(near[2:], axis=1) + jnp.concatenate(nexts[2:], axis=1)
    token_grad, gate_grad = finish(ids, gates, back, tokens.shape[1])
    return (token_grad, gate_grad.T, gate_wg[None], up_wg[None], down_wg.astype(BF)[None])


def solution(mesh):
    tok = P(("dp", "expert"), None)
    weight = P("expert", None, None)
    grad = P("expert", "dp", None)
    return jax.shard_map(
        per_device,
        mesh=mesh,
        in_specs=(tok, tok, tok, tok, weight, weight, weight),
        out_specs=(tok, tok, grad, grad, grad),
        check_vma=False,
    )
```

```python
import functools

import jax
import jax.numpy as jnp
from jax import lax
from jax.experimental import pallas as pl
from jax.experimental.pallas import tpu as pltpu
from jax.sharding import PartitionSpec as P

BF = jnp.bfloat16
F32 = jnp.float32
I32 = jnp.int32
CAP = 6
PAIRS = CAP // 2
EXPERTS = 64
EXT = 128
ROWS = EXPERTS * CAP
MIB = 1 << 20
SMEM_SPEC = pl.BlockSpec(memory_space=pltpu.SMEM)


def dot(a, b, dims):
    return lax.dot_general(a, b, (dims, ((), ())), preferred_element_type=F32)


def cost(flops, nbytes):
    return pl.CostEstimate(flops=flops, bytes_accessed=nbytes, transcendentals=0)


def whole(shape):
    return pl.BlockSpec(shape, lambda i: (0,) * len(shape))


def params():
    return pltpu.CompilerParams(vmem_limit_bytes=58 * MIB)


ANY_SPEC = pl.BlockSpec(memory_space=pl.ANY)


def fixed(x):
    return pltpu.with_memory_space_constraint(x, pltpu.HBM)


def iota(shape, dim):
    return lax.broadcasted_iota(I32, shape, dim)


def one_hot(hit):
    return jnp.where(hit, 1.0, 0.0).astype(BF)


def router(ids, gates, wide):
    k_top, tok = ids.shape
    rep = one_hot(iota((tok, wide), 0) == (iota((tok, wide), 1) & (tok - 1)))
    named_by = dot(ids[...].astype(F32).astype(BF), rep, ((1,), (0,)))
    gate_by = dot(gates[...], rep, ((1,), (0,)))
    shape = (EXPERTS, wide)
    e = iota(shape, 0).astype(F32)
    chosen = jnp.zeros(shape, F32)
    gate = jnp.zeros(shape, F32)
    for k in range(k_top):
        named = jnp.broadcast_to(named_by[k : k + 1, :], shape) == e
        chosen = jnp.where(named, 1.0, chosen)
        gate = jnp.where(named, jnp.broadcast_to(gate_by[k : k + 1, :], shape), gate)
    r, c = iota((wide, wide), 0), iota((wide, wide), 1)
    slot = dot(chosen.astype(BF), one_hot((r < c) & ((r >> 5) == (c >> 5))), ((1,), (0,)))
    return jnp.where(chosen > 0.0, slot + 1.0, 0.0), gate


def pack_kernel(ids, gates, tokens, grads, packed):
    tok, d = tokens.shape
    dq = d // 4
    wide = 8 * tok
    code, gate = router(ids, gates, wide)
    rows = packed.shape[0]
    own = one_hot((iota((rows, EXPERTS), 0) >> 4) == iota((rows, EXPERTS), 1))
    code = dot(own, code.astype(BF), ((1,), (0,)))
    gate = dot(own, gate.astype(BF), ((1,), (0,)))
    r, c = iota((rows, wide), 0), iota((rows, wide), 1)
    fits = (((r >> 3) & 1) == (c >> 7)) & ((r & 3) == ((c >> 5) & 3))
    value = jnp.where(c < 4 * tok, 1.0, gate)
    base = (((r >> 2) & 1) + 1).astype(F32)
    parts = [v[:, k * dq : (k + 1) * dq] for v in (tokens, grads) for k in range(4)]
    source = jnp.concatenate(parts, axis=0)
    for p in range(PAIRS):
        pick = jnp.where(fits & (code == base + 2.0 * p), value, 0.0).astype(BF)
        packed[:, p * dq : (p + 1) * dq] = dot(pick, source, ((1,), (0,))).astype(BF)


def pack(ids, gates, tokens, grads):
    tok, d = tokens.shape
    shape = (EXPERTS * 16, CAP * d // 8)
    ins = (ids, gates, tokens, grads)
    return pl.pallas_call(
        pack_kernel,
        grid=(1,),
        out_shape=pltpu.HBM(shape, BF),
        in_specs=[whole(v.shape) for v in ins],
        out_specs=whole(shape),
        compiler_params=params(),
        cost_estimate=cost(1 << 30, 4 * MIB),
        name="pack",
    )(*ins)


def put_down(ref, part, fq, width):
    top = ref.shape[0] - fq * 4 // 3
    third = fq // 3
    ref[top : top + fq, :] = part[:, :width]
    for i in range(3):
        cols = slice(i * width // 3, (i + 1) * width // 3)
        ref[top + fq :, cols] = part[i * third : (i + 1) * third, width:]


def gradient_part(ref, me, by, half, x_ref, s_ref, h4, g_ref):
    dq = x_ref.shape[1] // 4
    ff = g_ref.shape[1] // 2
    hd = s_ref.shape[1] // 2
    xq = x_ref[:, pl.ds(pl.multiple_of((me ^ by) * dq, dq), dq)]
    ref[:dq, :] = dot(xq, g_ref[:, half * ff : (half + 1) * ff], ((0,), (0,))).astype(BF)
    down = dot(h4[me ^ by], s_ref[:, half * hd : (half + 1) * hd], ((0,), (0,))).astype(BF)
    put_down(ref, down, h4.shape[2], ff)


def staged(refs, n_in, n_out):
    hbm_in, hbm_out = refs[:n_in], refs[n_in : n_in + n_out]
    vmem_in = refs[n_in + n_out : 2 * n_in + n_out]
    vmem_out = refs[2 * n_in + n_out : 2 * (n_in + n_out)]
    sems_in, sems_out = refs[2 * (n_in + n_out) :]
    loads = [pltpu.make_async_copy(h, v, sems_in.at[i]) for i, (h, v) in enumerate(zip(hbm_in, vmem_in))]
    stores = [pltpu.make_async_copy(v, h, sems_out.at[i]) for i, (h, v) in enumerate(zip(hbm_out, vmem_out))]
    for load in loads:
        load.start()
    return vmem_in, vmem_out, loads, stores


def staged_call(kernel, place, ins, shapes, limit, estimate, name):
    return pl.pallas_call(
        kernel,
        grid=(1,),
        out_shape=[pltpu.HBM(v, BF) for v in shapes],
        in_specs=[SMEM_SPEC] + [ANY_SPEC] * len(ins),
        out_specs=[ANY_SPEC] * len(shapes),
        scratch_shapes=[pltpu.VMEM(v.shape, BF) for v in ins]
        + [pltpu.VMEM(v, BF) for v in shapes]
        + [pltpu.SemaphoreType.DMA((len(ins),)), pltpu.SemaphoreType.DMA((len(shapes),))],
        compiler_params=pltpu.CompilerParams(vmem_limit_bytes=limit * MIB),
        cost_estimate=estimate,
        name=name,
    )(place, *ins)


def main_kernel(place, *refs):
    (got, wg, wu, wd), outs, loads, stores = staged(refs, 4, 9)
    back, x_ref, s_ref, h4, g_ref = outs[4:]
    d, ff = wg.shape
    dq, fq = d // 4, ff // 4
    o, c = iota((256, 256), 0), iota((256, 256), 1)
    i = o & 31
    unpick = one_hot(c == (i >> 1) * 16 + (o >> 7) * 8 + (i & 1) * 4 + ((o >> 5) & 3))
    loads[0].wait()
    for p in range(PAIRS):
        for b in range(4):
            part = dot(unpick, got[b * 256 : (b + 1) * 256, p * dq : (p + 1) * dq], ((1,), (0,))).astype(BF)
            rows = slice(p * 128 + b * 32, p * 128 + (b + 1) * 32)
            for k in range(4):
                x_ref[rows, k * dq : (k + 1) * dq] = part[k * 32 : (k + 1) * 32]
                s_ref[rows, k * dq : (k + 1) * dq] = part[128 + k * 32 : 128 + (k + 1) * 32]
    stores[5].start()
    stores[6].start()
    x = x_ref[...]
    loads[1].wait()
    a = dot(x, wg[...], ((1,), (0,)))
    loads[2].wait()
    u = dot(x, wu[...], ((1,), (0,)))
    loads[3].wait()
    gh = dot(s_ref[...], wd[...], ((1,), (1,)))
    sig = jax.nn.sigmoid(a)
    swish = a * sig
    hidden = (swish * u).astype(BF)
    g_ref[:, :ff] = (gh * (u * sig * (1.0 + a * (1.0 - sig)))).astype(BF)
    g_ref[:, ff:] = (gh * swish).astype(BF)
    for k in range(4):
        h4[k] = hidden[:, k * fq : (k + 1) * fq]
    stores[7].start()
    stores[8].start()
    me = place[0]
    for n, by, half in ((0, 2, 0), (1, 2, 1), (2, 1, 0), (3, 3, 1)):
        gradient_part(outs[n], me, by, half, x_ref, s_ref, h4, g_ref)
        stores[n].start()
    total = jnp.sum(gh * hidden.astype(F32), axis=1, keepdims=True)
    o, c = iota((128, 128), 0), iota((128, 128), 1)
    repick = one_hot(c == (o & 3) * 32 + (o >> 3) * 2 + ((o >> 2) & 1))
    parts = []
    for k in range(4):
        cols = slice(k * dq, (k + 1) * dq)
        part = dot(g_ref[:, :ff], wg[cols, :], ((1,), (1,))) + dot(g_ref[:, ff:], wu[cols, :], ((1,), (1,)))
        parts.append(part.astype(BF))
    for p in range(PAIRS):
        for b in range(4):
            rows = slice(p * 128 + b * 32, p * 128 + (b + 1) * 32)
            four = jnp.concatenate([part[rows] for part in parts], axis=0)
            back[b * 128 : (b + 1) * 128, p * dq : (p + 1) * dq] = dot(repick, four, ((1,), (0,))).astype(BF)
    lane = iota((128, EXT), 1)
    mixed = jnp.zeros((128, EXT), F32)
    for p in range(PAIRS):
        mixed = jnp.where(lane == p, total[p * 128 : (p + 1) * 128], mixed)
    o, c = iota((512, 128), 0), iota((512, 128), 1)
    spread = one_hot((c == (o >> 3) * 2 + ((o >> 2) & 1)) & ((o & 3) == 0))
    back[:, PAIRS * dq :] = dot(spread, mixed.astype(BF), ((1,), (0,))).astype(BF)
    stores[4].start()
    for store in stores:
        store.wait()


def main_rows(place, got, wg, wu, wd):
    d, ff = wg.shape
    packed = (d // 4 + ff // 3, ff)
    shapes = [packed] * 4 + [(EXPERTS * 8, CAP * d // 8 + EXT)]
    shapes += [(ROWS, d), (ROWS, d), (4, ROWS, ff // 4), (ROWS, 2 * ff)]
    ins = (got, fixed(wg), fixed(wu), fixed(wd))
    return staged_call(main_kernel, place, ins, shapes, 46, cost(14 * ROWS * d * ff, 24 * MIB), "main_rows")


def next_kernel(place, *refs):
    (x_ref, s_ref, h4, g_ref, far1, far3), outs, loads, stores = staged(refs, 6, 4)
    for load in loads:
        load.wait()
    me = place[0]
    for n, by, half, got in ((0, 3, 0, far1), (1, 1, 1, far3), (2, 0, 0, None), (3, 0, 1, None)):
        gradient_part(outs[n], me, by, half, x_ref, s_ref, h4, g_ref)
        if got is not None:
            outs[n][...] = (outs[n][...].astype(F32) + got[...].astype(F32)).astype(BF)
        stores[n].start()
    for store in stores:
        store.wait()


def next_parts(place, x, s, h4, g, far1, far3):
    ins = (x, s, h4, g, far1, far3)
    estimate = cost(3 * ROWS * x.shape[1] * g.shape[1] // 2, 13 * MIB)
    return staged_call(next_kernel, place, ins, [far1.shape] * 4, 58, estimate, "next_parts")


def close_kernel(kept1, kept3, next1, next3, gate, up, down):
    dq, ff = gate.shape
    fq, d = down.shape
    third = fq // 3
    for half, (kept, got, out) in enumerate(((kept1, next1, gate), (kept3, next3, up))):
        total = (kept[...].astype(F32) + got[...].astype(F32)).astype(BF)
        out[...] = total[:dq]
        left = half * d // 2
        down[:, left : left + ff] = total[dq : dq + fq]
        for i in range(3):
            cols = slice(i * ff // 3, (i + 1) * ff // 3)
            down[i * third : (i + 1) * third, left + ff : left + d // 2] = total[dq + fq :, cols]


def close(kept, nexts, d):
    rows, ff = kept[0].shape
    shapes = [(d // 4, ff)] * 2 + [(ff // 4, d)]
    ins = (*kept, *nexts)
    return pl.pallas_call(
        close_kernel,
        grid=(1,),
        out_shape=[jax.ShapeDtypeStruct(v, BF) for v in shapes],
        in_specs=[whole(v.shape) for v in ins],
        out_specs=[whole(v) for v in shapes],
        compiler_params=pltpu.CompilerParams(vmem_limit_bytes=24 * MIB),
        cost_estimate=cost(1 << 21, 7 * MIB),
        name="close",
    )(*ins)


def finish_kernel(ids, gates, got, token_grad, gate_grad):
    k_top, tok = ids.shape
    wide = 4 * tok
    dq = token_grad.shape[1] // 4
    n = got.shape[0]
    code, _ = router(ids, gates, wide)
    from_e = one_hot(iota((EXPERTS, n), 0) == (iota((EXPERTS, n), 1) >> 3))
    code_cols = dot(code.astype(BF), from_e, ((0,), (0,)))
    r, c = iota((wide, n), 0), iota((wide, n), 1)
    fits = (r >> 5) == (c & 3)
    base = (((c >> 2) & 1) + 1).astype(F32)
    total = None
    for p in range(PAIRS):
        pick = one_hot(fits & (code_cols == base + 2.0 * p))
        part = dot(pick, got[:, p * dq : (p + 1) * dq], ((1,), (0,)))
        total = part if total is None else total + part
    for k in range(4):
        token_grad[:, k * dq : (k + 1) * dq] = total[k * tok : (k + 1) * tok].astype(BF)

    code = code[:, :tok]
    by_slot = jnp.zeros((EXPERTS, tok), F32)
    r, c = iota((EXPERTS, n), 0), iota((EXPERTS, n), 1)
    for parity in range(2):
        at = one_hot(c == r * 8 + 4 * parity)
        values = dot(at, got[:, PAIRS * dq :], ((1,), (0,)))
        for p in range(PAIRS):
            by_slot = jnp.where(code == 2.0 * p + parity + 1.0, values[:, p : p + 1], by_slot)
    e = iota((EXPERTS, tok), 0)
    rows = []
    for k in range(k_top):
        named = jnp.broadcast_to(ids[k : k + 1, :], (EXPERTS, tok)) == e
        rows.append(jnp.sum(jnp.where(named, by_slot, 0.0), axis=0, keepdims=True))
    gate_grad[...] = (jnp.concatenate(rows, axis=0) / gates[...].astype(F32)).astype(BF)


def finish(ids, gates, got, d):
    out = (ids.shape[1], d)
    ins = (ids, gates, got)
    return pl.pallas_call(
        finish_kernel,
        grid=(1,),
        out_shape=[jax.ShapeDtypeStruct(out, BF), jax.ShapeDtypeStruct(ids.shape, BF)],
        in_specs=[whole(v.shape) for v in ins],
        out_specs=[whole(out), whole(ids.shape)],
        compiler_params=pltpu.CompilerParams(vmem_limit_bytes=24 * MIB),
        cost_estimate=cost(1 << 28, 2 * MIB),
        name="finish",
    )(*ins)


def swap(v, by):
    return lax.ppermute(v, "dp", [(i, i ^ by) for i in range(4)])


def exchange(v):
    shape = (EXPERTS, v.shape[0] // EXPERTS, v.shape[1])
    return lax.all_to_all(v.reshape(shape), "expert", split_axis=0, concat_axis=0, tiled=True).reshape(v.shape)


def plus(a, b):
    return (a.astype(F32) + b.astype(F32)).astype(BF)


def per_device(tokens, grad_out, expert_ids, gate_values, w_gate, w_up, w_down):
    features = tokens.shape[1]
    place = lax.axis_index("dp").astype(I32).reshape(1)
    ids, gates = expert_ids.T, gate_values.T
    wg, wu, wd = w_gate[0], w_up[0], w_down[0]
    got = exchange(pack(ids, gates, tokens, grad_out))
    far1, far3, near1, near3, back, x, s, h4, g = main_rows(place, got, wg, wu, wd)
    far1, far3 = swap(far1, 1), swap(far3, 3)
    near1, near3 = swap(near1, 1), swap(near3, 3)
    back = exchange(back)
    next1, next3, own1, own3 = next_parts(place, x, s, h4, g, far1, far3)
    next1, next3 = swap(next1, 3), swap(next3, 1)
    kept = plus(own1, near1), plus(own3, near3)
    gate_wg, up_wg, down_wg = close(kept, (next1, next3), features)
    token_grad, gate_grad = finish(ids, gates, back, features)
    return (token_grad, gate_grad.T, gate_wg[None], up_wg[None], down_wg[None])


def solution(mesh):
    tok = P(("dp", "expert"), None)
    weight = P("expert", None, None)
    grad = P("expert", "dp", None)
    return jax.shard_map(
        per_device,
        mesh=mesh,
        in_specs=(tok, tok, tok, tok, weight, weight, weight),
        out_specs=(tok, tok, grad, grad, grad),
        check_vma=False,
    )
```

```python
import functools

import jax
import jax.numpy as jnp
from jax import lax
from jax.experimental import pallas as pl
from jax.experimental.pallas import tpu as pltpu
from jax.sharding import PartitionSpec as P

BF = jnp.bfloat16
F32 = jnp.float32
I32 = jnp.int32
CAP = 6
PAIRS = CAP // 2
EXPERTS = 64
EXT = 128
ROWS = EXPERTS * CAP
MIB = 1 << 20
SMEM_SPEC = pl.BlockSpec(memory_space=pltpu.SMEM)


def dot(a, b, dims):
    return lax.dot_general(a, b, (dims, ((), ())), preferred_element_type=F32)


def cost(flops, nbytes):
    return pl.CostEstimate(flops=flops, bytes_accessed=nbytes, transcendentals=0)


def whole(shape):
    return pl.BlockSpec(shape, lambda i: (0,) * len(shape))


def params():
    return pltpu.CompilerParams(vmem_limit_bytes=58 * MIB)


ANY_SPEC = pl.BlockSpec(memory_space=pl.ANY)


def fixed(x):
    return pltpu.with_memory_space_constraint(x, pltpu.HBM)


def iota(shape, dim):
    return lax.broadcasted_iota(I32, shape, dim)


def one_hot(hit):
    return jnp.where(hit, 1.0, 0.0).astype(BF)


def router(ids, gates, wide):
    k_top, tok = ids.shape
    rep = one_hot(iota((tok, wide), 0) == (iota((tok, wide), 1) & (tok - 1)))
    named_by = dot(ids[...].astype(F32).astype(BF), rep, ((1,), (0,)))
    gate_by = dot(gates[...], rep, ((1,), (0,)))
    shape = (EXPERTS, wide)
    e = iota(shape, 0).astype(F32)
    chosen = jnp.zeros(shape, F32)
    gate = jnp.zeros(shape, F32)
    for k in range(k_top):
        named = jnp.broadcast_to(named_by[k : k + 1, :], shape) == e
        chosen = jnp.where(named, 1.0, chosen)
        gate = jnp.where(named, jnp.broadcast_to(gate_by[k : k + 1, :], shape), gate)
    r, c = iota((wide, wide), 0), iota((wide, wide), 1)
    slot = dot(chosen.astype(BF), one_hot((r < c) & ((r >> 5) == (c >> 5))), ((1,), (0,)))
    return jnp.where(chosen > 0.0, slot + 1.0, 0.0), gate


def pack_kernel(ids, gates, tokens, grads, packed):
    tok, d = tokens.shape
    dq = d // 4
    wide = 8 * tok
    code, gate = router(ids, gates, wide)
    rows = packed.shape[0]
    own = one_hot((iota((rows, EXPERTS), 0) >> 4) == iota((rows, EXPERTS), 1))
    code = dot(own, code.astype(BF), ((1,), (0,)))
    gate = dot(own, gate.astype(BF), ((1,), (0,)))
    r, c = iota((rows, wide), 0), iota((rows, wide), 1)
    fits = (((r >> 3) & 1) == (c >> 7)) & ((r & 3) == ((c >> 5) & 3))
    value = jnp.where(c < 4 * tok, 1.0, gate)
    base = (((r >> 2) & 1) + 1).astype(F32)
    parts = [v[:, k * dq : (k + 1) * dq] for v in (tokens, grads) for k in range(4)]
    source = jnp.concatenate(parts, axis=0)
    for p in range(PAIRS):
        pick = jnp.where(fits & (code == base + 2.0 * p), value, 0.0).astype(BF)
        packed[:, p * dq : (p + 1) * dq] = dot(pick, source, ((1,), (0,))).astype(BF)


def pack(ids, gates, tokens, grads):
    tok, d = tokens.shape
    shape = (EXPERTS * 16, CAP * d // 8)
    ins = (ids, gates, tokens, grads)
    return pl.pallas_call(
        pack_kernel,
        grid=(1,),
        out_shape=pltpu.HBM(shape, BF),
        in_specs=[whole(v.shape) for v in ins],
        out_specs=whole(shape),
        compiler_params=params(),
        cost_estimate=cost(1 << 30, 4 * MIB),
        name="pack",
    )(*ins)


def gradient_part(me, by, half, x_ref, g_ref):
    dq = x_ref.shape[1] // 4
    ff = g_ref.shape[1] // 2
    xq = x_ref[:, pl.ds(pl.multiple_of((me ^ by) * dq, dq), dq)]
    return dot(xq, g_ref[:, half * ff : (half + 1) * ff], ((0,), (0,)))


def staged(refs, n_in, n_out):
    hbm_in, hbm_out = refs[:n_in], refs[n_in : n_in + n_out]
    vmem_in = refs[n_in + n_out : 2 * n_in + n_out]
    vmem_out = refs[2 * n_in + n_out : 2 * (n_in + n_out)]
    sems_in, sems_out = refs[2 * (n_in + n_out) : 2 * (n_in + n_out) + 2]
    loads = [pltpu.make_async_copy(h, v, sems_in.at[i]) for i, (h, v) in enumerate(zip(hbm_in, vmem_in))]
    stores = [pltpu.make_async_copy(v, h, sems_out.at[i]) for i, (h, v) in enumerate(zip(hbm_out, vmem_out))]
    for load in loads:
        load.start()
    return vmem_in, vmem_out, loads, stores


def staged_call(kernel, place, ins, shapes, limit, estimate, name, scratch=()):
    return pl.pallas_call(
        kernel,
        grid=(1,),
        out_shape=[pltpu.HBM(v, BF) for v in shapes],
        in_specs=[SMEM_SPEC] + [ANY_SPEC] * len(ins),
        out_specs=[ANY_SPEC] * len(shapes),
        scratch_shapes=[pltpu.VMEM(v.shape, BF) for v in ins]
        + [pltpu.VMEM(v, BF) for v in shapes]
        + [pltpu.SemaphoreType.DMA((len(ins),)), pltpu.SemaphoreType.DMA((len(shapes),))]
        + [pltpu.VMEM(v, BF) for v in scratch],
        compiler_params=pltpu.CompilerParams(vmem_limit_bytes=limit * MIB),
        cost_estimate=estimate,
        name=name,
    )(place, *ins)


def main_kernel(place, *refs):
    (got, wg, wu, wd), outs, loads, stores = staged(refs, 4, 8)
    down, back, x_ref, g_ref = outs[4:]
    s_ref = refs[-1]
    d, ff = wg.shape
    dq = d // 4
    o, c = iota((256, 256), 0), iota((256, 256), 1)
    i = o & 31
    unpick = one_hot(c == (i >> 1) * 16 + (o >> 7) * 8 + (i & 1) * 4 + ((o >> 5) & 3))
    loads[0].wait()
    for p in range(PAIRS):
        for b in range(4):
            part = dot(unpick, got[b * 256 : (b + 1) * 256, p * dq : (p + 1) * dq], ((1,), (0,))).astype(BF)
            rows = slice(p * 128 + b * 32, p * 128 + (b + 1) * 32)
            for k in range(4):
                x_ref[rows, k * dq : (k + 1) * dq] = part[k * 32 : (k + 1) * 32]
                s_ref[rows, k * dq : (k + 1) * dq] = part[128 + k * 32 : 128 + (k + 1) * 32]
    stores[6].start()
    x = x_ref[...]
    loads[1].wait()
    a = dot(x, wg[...], ((1,), (0,)))
    loads[2].wait()
    u = dot(x, wu[...], ((1,), (0,)))
    loads[3].wait()
    gh = dot(s_ref[...], wd[...], ((1,), (1,)))
    sig = jax.nn.sigmoid(a)
    swish = a * sig
    hidden = (swish * u).astype(BF)
    g_ref[:, :ff] = (gh * (u * sig * (1.0 + a * (1.0 - sig)))).astype(BF)
    g_ref[:, ff:] = (gh * swish).astype(BF)
    stores[7].start()
    for j in range(0, d, dq):
        down[:, j : j + dq] = dot(hidden, s_ref[:, j : j + dq], ((0,), (0,))).astype(BF)
    stores[4].start()
    me = place[0]
    for n, by, half in ((0, 2, 0), (1, 2, 1), (2, 1, 0), (3, 3, 1)):
        outs[n][...] = gradient_part(me, by, half, x_ref, g_ref).astype(BF)
        stores[n].start()
    total = jnp.sum(gh * hidden.astype(F32), axis=1, keepdims=True)
    o, c = iota((128, 128), 0), iota((128, 128), 1)
    repick = one_hot(c == (o & 3) * 32 + (o >> 3) * 2 + ((o >> 2) & 1))
    parts = []
    for k in range(4):
        cols = slice(k * dq, (k + 1) * dq)
        part = dot(g_ref[:, :ff], wg[cols, :], ((1,), (1,))) + dot(g_ref[:, ff:], wu[cols, :], ((1,), (1,)))
        parts.append(part.astype(BF))
    for p in range(PAIRS):
        for b in range(4):
            rows = slice(p * 128 + b * 32, p * 128 + (b + 1) * 32)
            four = jnp.concatenate([part[rows] for part in parts], axis=0)
            back[b * 128 : (b + 1) * 128, p * dq : (p + 1) * dq] = dot(repick, four, ((1,), (0,))).astype(BF)
    lane = iota((128, EXT), 1)
    mixed = jnp.zeros((128, EXT), F32)
    for p in range(PAIRS):
        mixed = jnp.where(lane == p, total[p * 128 : (p + 1) * 128], mixed)
    o, c = iota((512, 128), 0), iota((512, 128), 1)
    spread = one_hot((c == (o >> 3) * 2 + ((o >> 2) & 1)) & ((o & 3) == 0))
    back[:, PAIRS * dq :] = dot(spread, mixed.astype(BF), ((1,), (0,))).astype(BF)
    stores[5].start()
    for store in stores:
        store.wait()


def main_rows(place, got, wg, wu, wd):
    d, ff = wg.shape
    shapes = [(d // 4, ff)] * 4 + [(ff, d), (EXPERTS * 8, CAP * d // 8 + EXT), (ROWS, d), (ROWS, 2 * ff)]
    ins = (got, fixed(wg), fixed(wu), fixed(wd))
    estimate = cost(15 * ROWS * d * ff, 24 * MIB)
    return staged_call(main_kernel, place, ins, shapes, 46, estimate, "main_rows", [(ROWS, d)])


def next_kernel(place, *refs):
    (x_ref, g_ref, far1, far3), outs, loads, stores = staged(refs, 4, 4)
    loads[0].wait()
    loads[1].wait()
    me = place[0]
    for n, by, half, got in ((0, 3, 0, far1), (1, 1, 1, far3), (2, 0, 0, None), (3, 0, 1, None)):
        part = gradient_part(me, by, half, x_ref, g_ref)
        if got is not None:
            loads[2 + n].wait()
            part = part + got[...].astype(F32)
        outs[n][...] = part.astype(BF)
        stores[n].start()
    for store in stores:
        store.wait()


def next_parts(place, x, g, far1, far3):
    ins = (x, g, far1, far3)
    estimate = cost(2 * ROWS * x.shape[1] * g.shape[1] // 2, 8 * MIB)
    return staged_call(next_kernel, place, ins, [far1.shape] * 4, 58, estimate, "next_parts")


def finish_kernel(ids, gates, got, token_grad, gate_grad):
    k_top, tok = ids.shape
    wide = 4 * tok
    dq = token_grad.shape[1] // 4
    n = got.shape[0]
    code, _ = router(ids, gates, wide)
    from_e = one_hot(iota((EXPERTS, n), 0) == (iota((EXPERTS, n), 1) >> 3))
    code_cols = dot(code.astype(BF), from_e, ((0,), (0,)))
    r, c = iota((wide, n), 0), iota((wide, n), 1)
    fits = (r >> 5) == (c & 3)
    base = (((c >> 2) & 1) + 1).astype(F32)
    total = None
    for p in range(PAIRS):
        pick = one_hot(fits & (code_cols == base + 2.0 * p))
        part = dot(pick, got[:, p * dq : (p + 1) * dq], ((1,), (0,)))
        total = part if total is None else total + part
    for k in range(4):
        token_grad[:, k * dq : (k + 1) * dq] = total[k * tok : (k + 1) * tok].astype(BF)

    code = code[:, :tok]
    by_slot = jnp.zeros((EXPERTS, tok), F32)
    r, c = iota((EXPERTS, n), 0), iota((EXPERTS, n), 1)
    for parity in range(2):
        at = one_hot(c == r * 8 + 4 * parity)
        values = dot(at, got[:, PAIRS * dq :], ((1,), (0,)))
        for p in range(PAIRS):
            by_slot = jnp.where(code == 2.0 * p + parity + 1.0, values[:, p : p + 1], by_slot)
    e = iota((EXPERTS, tok), 0)
    rows = []
    for k in range(k_top):
        named = jnp.broadcast_to(ids[k : k + 1, :], (EXPERTS, tok)) == e
        rows.append(jnp.sum(jnp.where(named, by_slot, 0.0), axis=0, keepdims=True))
    gate_grad[...] = (jnp.concatenate(rows, axis=0) / gates[...].astype(F32)).astype(BF)


def finish(ids, gates, got, d):
    out = (ids.shape[1], d)
    ins = (ids, gates, got)
    return pl.pallas_call(
        finish_kernel,
        grid=(1,),
        out_shape=[jax.ShapeDtypeStruct(out, BF), jax.ShapeDtypeStruct(ids.shape, BF)],
        in_specs=[whole(v.shape) for v in ins],
        out_specs=[whole(out), whole(ids.shape)],
        compiler_params=pltpu.CompilerParams(vmem_limit_bytes=24 * MIB),
        cost_estimate=cost(1 << 28, 2 * MIB),
        name="finish",
    )(*ins)


def swap(v, by):
    return lax.ppermute(v, "dp", [(i, i ^ by) for i in range(4)])


def exchange(v):
    shape = (EXPERTS, v.shape[0] // EXPERTS, v.shape[1])
    return lax.all_to_all(v.reshape(shape), "expert", split_axis=0, concat_axis=0, tiled=True).reshape(v.shape)


def plus(a, b):
    return (a.astype(F32) + b.astype(F32)).astype(BF)


def per_device(tokens, grad_out, expert_ids, gate_values, w_gate, w_up, w_down):
    features = tokens.shape[1]
    place = lax.axis_index("dp").astype(I32).reshape(1)
    ids, gates = expert_ids.T, gate_values.T
    wg, wu, wd = w_gate[0], w_up[0], w_down[0]
    got = exchange(pack(ids, gates, tokens, grad_out))
    far1, far3, near1, near3, down, back, x, g = main_rows(place, got, wg, wu, wd)
    down_wg = lax.psum_scatter(down, "dp", scatter_dimension=0, tiled=True)
    far1, far3 = swap(far1, 1), swap(far3, 3)
    near1, near3 = swap(near1, 1), swap(near3, 3)
    back = exchange(back)
    next1, next3, own1, own3 = next_parts(place, x, g, far1, far3)
    next1, next3 = swap(next1, 3), swap(next3, 1)
    gate_wg = plus(plus(own1, near1), next1)
    up_wg = plus(plus(own3, near3), next3)
    token_grad, gate_grad = finish(ids, gates, back, features)
    return (token_grad, gate_grad.T, gate_wg[None], up_wg[None], down_wg[None])


def solution(mesh):
    tok = P(("dp", "expert"), None)
    weight = P("expert", None, None)
    grad = P("expert", "dp", None)
    return jax.shard_map(
        per_device,
        mesh=mesh,
        in_specs=(tok, tok, tok, tok, weight, weight, weight),
        out_specs=(tok, tok, grad, grad, grad),
        check_vma=False,
    )
```

```python
import functools

import jax
import jax.numpy as jnp
from jax import lax
from jax.experimental import pallas as pl
from jax.experimental.pallas import tpu as pltpu
from jax.sharding import PartitionSpec as P

BF = jnp.bfloat16
F32 = jnp.float32
I32 = jnp.int32
CAP = 6
PAIRS = CAP // 2
EXPERTS = 64
EXT = 128
ROWS = EXPERTS * CAP
MIB = 1 << 20
SMEM_SPEC = pl.BlockSpec(memory_space=pltpu.SMEM)


def dot(a, b, dims):
    return lax.dot_general(a, b, (dims, ((), ())), preferred_element_type=F32)


def cost(flops, nbytes):
    return pl.CostEstimate(flops=flops, bytes_accessed=nbytes, transcendentals=0)


def whole(shape):
    return pl.BlockSpec(shape, lambda i: (0,) * len(shape))


def params():
    return pltpu.CompilerParams(vmem_limit_bytes=58 * MIB)


ANY_SPEC = pl.BlockSpec(memory_space=pl.ANY)


def fixed(x):
    return pltpu.with_memory_space_constraint(x, pltpu.HBM)


def iota(shape, dim):
    return lax.broadcasted_iota(I32, shape, dim)


def one_hot(hit):
    return jnp.where(hit, 1.0, 0.0).astype(BF)


def router(ids, gates, wide):
    k_top, tok = ids.shape
    rep = one_hot(iota((tok, wide), 0) == (iota((tok, wide), 1) & (tok - 1)))
    named_by = dot(ids[...].astype(F32).astype(BF), rep, ((1,), (0,)))
    gate_by = dot(gates[...], rep, ((1,), (0,)))
    shape = (EXPERTS, wide)
    e = iota(shape, 0).astype(F32)
    chosen = jnp.zeros(shape, F32)
    gate = jnp.zeros(shape, F32)
    for k in range(k_top):
        named = jnp.broadcast_to(named_by[k : k + 1, :], shape) == e
        chosen = jnp.where(named, 1.0, chosen)
        gate = jnp.where(named, jnp.broadcast_to(gate_by[k : k + 1, :], shape), gate)
    r, c = iota((wide, wide), 0), iota((wide, wide), 1)
    slot = dot(chosen.astype(BF), one_hot((r < c) & ((r >> 5) == (c >> 5))), ((1,), (0,)))
    return jnp.where(chosen > 0.0, slot + 1.0, 0.0), gate


def pack_kernel(ids, gates, tokens, grads, packed):
    tok, d = tokens.shape
    dq = d // 4
    wide = 8 * tok
    code, gate = router(ids, gates, wide)
    rows = packed.shape[0]
    own = one_hot((iota((rows, EXPERTS), 0) >> 4) == iota((rows, EXPERTS), 1))
    code = dot(own, code.astype(BF), ((1,), (0,)))
    gate = dot(own, gate.astype(BF), ((1,), (0,)))
    r, c = iota((rows, wide), 0), iota((rows, wide), 1)
    fits = (((r >> 3) & 1) == (c >> 7)) & ((r & 3) == ((c >> 5) & 3))
    value = jnp.where(c < 4 * tok, 1.0, gate)
    base = (((r >> 2) & 1) + 1).astype(F32)
    parts = [v[:, k * dq : (k + 1) * dq] for v in (tokens, grads) for k in range(4)]
    source = jnp.concatenate(parts, axis=0)
    for p in range(PAIRS):
        pick = jnp.where(fits & (code == base + 2.0 * p), value, 0.0).astype(BF)
        packed[:, p * dq : (p + 1) * dq] = dot(pick, source, ((1,), (0,))).astype(BF)


def pack(ids, gates, tokens, grads):
    tok, d = tokens.shape
    shape = (EXPERTS * 16, CAP * d // 8)
    ins = (ids, gates, tokens, grads)
    return pl.pallas_call(
        pack_kernel,
        grid=(1,),
        out_shape=pltpu.HBM(shape, BF),
        in_specs=[whole(v.shape) for v in ins],
        out_specs=whole(shape),
        compiler_params=params(),
        cost_estimate=cost(1 << 30, 4 * MIB),
        name="pack",
    )(*ins)


def put_down(ref, part, fq, width):
    top = ref.shape[0] - fq * 4 // 3
    third = fq // 3
    ref[top : top + fq, :] = part[:, :width]
    for i in range(3):
        cols = slice(i * width // 3, (i + 1) * width // 3)
        ref[top + fq :, cols] = part[i * third : (i + 1) * third, width:]


def gradient_part(ref, me, by, half, x_ref, s_ref, h4, g_ref):
    dq = x_ref.shape[1] // 4
    ff = g_ref.shape[1] // 2
    hd = s_ref.shape[1] // 2
    xq = x_ref[:, pl.ds(pl.multiple_of((me ^ by) * dq, dq), dq)]
    ref[:dq, :] = dot(xq, g_ref[:, half * ff : (half + 1) * ff], ((0,), (0,))).astype(BF)
    down = dot(h4[me ^ by], s_ref[:, half * hd : (half + 1) * hd], ((0,), (0,))).astype(BF)
    put_down(ref, down, h4.shape[2], ff)


def staged(refs, n_in, n_out):
    hbm_in, hbm_out = refs[:n_in], refs[n_in : n_in + n_out]
    vmem_in = refs[n_in + n_out : 2 * n_in + n_out]
    vmem_out = refs[2 * n_in + n_out : 2 * (n_in + n_out)]
    sems_in, sems_out = refs[2 * (n_in + n_out) :]
    loads = [pltpu.make_async_copy(h, v, sems_in.at[i]) for i, (h, v) in enumerate(zip(hbm_in, vmem_in))]
    stores = [pltpu.make_async_copy(v, h, sems_out.at[i]) for i, (h, v) in enumerate(zip(hbm_out, vmem_out))]
    for load in loads:
        load.start()
    return vmem_in, vmem_out, loads, stores


def staged_call(kernel, place, ins, shapes, limit, estimate, name):
    return pl.pallas_call(
        kernel,
        grid=(1,),
        out_shape=[pltpu.HBM(v, BF) for v in shapes],
        in_specs=[SMEM_SPEC] + [ANY_SPEC] * len(ins),
        out_specs=[ANY_SPEC] * len(shapes),
        scratch_shapes=[pltpu.VMEM(v.shape, BF) for v in ins]
        + [pltpu.VMEM(v, BF) for v in shapes]
        + [pltpu.SemaphoreType.DMA((len(ins),)), pltpu.SemaphoreType.DMA((len(shapes),))],
        compiler_params=pltpu.CompilerParams(vmem_limit_bytes=limit * MIB),
        cost_estimate=estimate,
        name=name,
    )(place, *ins)


def main_kernel(place, *refs):
    (got, wg, wu, wd), outs, loads, stores = staged(refs, 4, 9)
    back, x_ref, s_ref, h4, g_ref = outs[4:]
    d, ff = wg.shape
    dq, fq = d // 4, ff // 4
    o, c = iota((256, 256), 0), iota((256, 256), 1)
    i = o & 31
    unpick = one_hot(c == (i >> 1) * 16 + (o >> 7) * 8 + (i & 1) * 4 + ((o >> 5) & 3))
    loads[0].wait()
    for p in range(PAIRS):
        for b in range(4):
            part = dot(unpick, got[b * 256 : (b + 1) * 256, p * dq : (p + 1) * dq], ((1,), (0,))).astype(BF)
            rows = slice(p * 128 + b * 32, p * 128 + (b + 1) * 32)
            for k in range(4):
                x_ref[rows, k * dq : (k + 1) * dq] = part[k * 32 : (k + 1) * 32]
                s_ref[rows, k * dq : (k + 1) * dq] = part[128 + k * 32 : 128 + (k + 1) * 32]
    stores[5].start()
    stores[6].start()
    x = x_ref[...]
    loads[1].wait()
    a = dot(x, wg[...], ((1,), (0,)))
    loads[2].wait()
    u = dot(x, wu[...], ((1,), (0,)))
    loads[3].wait()
    gh = dot(s_ref[...], wd[...], ((1,), (1,)))
    sig = jax.nn.sigmoid(a)
    swish = a * sig
    hidden = (swish * u).astype(BF)
    g_ref[:, :ff] = (gh * (u * sig * (1.0 + a * (1.0 - sig)))).astype(BF)
    g_ref[:, ff:] = (gh * swish).astype(BF)
    for k in range(4):
        h4[k] = hidden[:, k * fq : (k + 1) * fq]
    stores[7].start()
    stores[8].start()
    me = place[0]
    for n, by, half in ((0, 2, 0), (1, 2, 1), (2, 1, 0), (3, 3, 1)):
        gradient_part(outs[n], me, by, half, x_ref, s_ref, h4, g_ref)
        stores[n].start()
    total = jnp.sum(gh * hidden.astype(F32), axis=1, keepdims=True)
    o, c = iota((128, 128), 0), iota((128, 128), 1)
    repick = one_hot(c == (o & 3) * 32 + (o >> 3) * 2 + ((o >> 2) & 1))
    parts = []
    for k in range(4):
        cols = slice(k * dq, (k + 1) * dq)
        part = dot(g_ref[:, :ff], wg[cols, :], ((1,), (1,))) + dot(g_ref[:, ff:], wu[cols, :], ((1,), (1,)))
        parts.append(part.astype(BF))
    for p in range(PAIRS):
        for b in range(4):
            rows = slice(p * 128 + b * 32, p * 128 + (b + 1) * 32)
            four = jnp.concatenate([part[rows] for part in parts], axis=0)
            back[b * 128 : (b + 1) * 128, p * dq : (p + 1) * dq] = dot(repick, four, ((1,), (0,))).astype(BF)
    lane = iota((128, EXT), 1)
    mixed = jnp.zeros((128, EXT), F32)
    for p in range(PAIRS):
        mixed = jnp.where(lane == p, total[p * 128 : (p + 1) * 128], mixed)
    o, c = iota((512, 128), 0), iota((512, 128), 1)
    spread = one_hot((c == (o >> 3) * 2 + ((o >> 2) & 1)) & ((o & 3) == 0))
    back[:, PAIRS * dq :] = dot(spread, mixed.astype(BF), ((1,), (0,))).astype(BF)
    stores[4].start()
    for store in stores:
        store.wait()


def main_rows(place, got, wg, wu, wd):
    d, ff = wg.shape
    packed = (d // 4 + ff // 3, ff)
    shapes = [packed] * 4 + [(EXPERTS * 8, CAP * d // 8 + EXT)]
    shapes += [(ROWS, d), (ROWS, d), (4, ROWS, ff // 4), (ROWS, 2 * ff)]
    ins = (got, fixed(wg), fixed(wu), fixed(wd))
    return staged_call(main_kernel, place, ins, shapes, 46, cost(14 * ROWS * d * ff, 24 * MIB), "main_rows")


def next_kernel(place, *refs):
    (x_ref, s_ref, h4, g_ref, far1, far3), outs, loads, stores = staged(refs, 6, 4)
    for load in loads:
        load.wait()
    me = place[0]
    for n, by, half, got in ((0, 3, 0, far1), (1, 1, 1, far3), (2, 0, 0, None), (3, 0, 1, None)):
        gradient_part(outs[n], me, by, half, x_ref, s_ref, h4, g_ref)
        if got is not None:
            outs[n][...] = (outs[n][...].astype(F32) + got[...].astype(F32)).astype(BF)
        stores[n].start()
    for store in stores:
        store.wait()


def next_parts(place, x, s, h4, g, far1, far3):
    ins = (x, s, h4, g, far1, far3)
    estimate = cost(60 * ROWS * x.shape[1] * g.shape[1] // 2, 13 * MIB)
    return staged_call(next_kernel, place, ins, [far1.shape] * 4, 58, estimate, "next_parts")


def close_kernel(kept1, kept3, next1, next3, gate, up, down):
    dq, ff = gate.shape
    fq, d = down.shape
    third = fq // 3
    for half, (kept, got, out) in enumerate(((kept1, next1, gate), (kept3, next3, up))):
        total = (kept[...].astype(F32) + got[...].astype(F32)).astype(BF)
        out[...] = total[:dq]
        left = half * d // 2
        down[:, left : left + ff] = total[dq : dq + fq]
        for i in range(3):
            cols = slice(i * ff // 3, (i + 1) * ff // 3)
            down[i * third : (i + 1) * third, left + ff : left + d // 2] = total[dq + fq :, cols]


def close(kept, nexts, d):
    rows, ff = kept[0].shape
    shapes = [(d // 4, ff)] * 2 + [(ff // 4, d)]
    ins = (*kept, *nexts)
    return pl.pallas_call(
        close_kernel,
        grid=(1,),
        out_shape=[jax.ShapeDtypeStruct(v, BF) for v in shapes],
        in_specs=[whole(v.shape) for v in ins],
        out_specs=[whole(v) for v in shapes],
        compiler_params=pltpu.CompilerParams(vmem_limit_bytes=24 * MIB),
        cost_estimate=cost(1 << 21, 7 * MIB),
        name="close",
    )(*ins)


def finish_kernel(ids, gates, got, token_grad, gate_grad):
    k_top, tok = ids.shape
    wide = 4 * tok
    dq = token_grad.shape[1] // 4
    n = got.shape[0]
    code, _ = router(ids, gates, wide)
    from_e = one_hot(iota((EXPERTS, n), 0) == (iota((EXPERTS, n), 1) >> 3))
    code_cols = dot(code.astype(BF), from_e, ((0,), (0,)))
    r, c = iota((wide, n), 0), iota((wide, n), 1)
    fits = (r >> 5) == (c & 3)
    base = (((c >> 2) & 1) + 1).astype(F32)
    total = None
    for p in range(PAIRS):
        pick = one_hot(fits & (code_cols == base + 2.0 * p))
        part = dot(pick, got[:, p * dq : (p + 1) * dq], ((1,), (0,)))
        total = part if total is None else total + part
    for k in range(4):
        token_grad[:, k * dq : (k + 1) * dq] = total[k * tok : (k + 1) * tok].astype(BF)

    code = code[:, :tok]
    by_slot = jnp.zeros((EXPERTS, tok), F32)
    r, c = iota((EXPERTS, n), 0), iota((EXPERTS, n), 1)
    for parity in range(2):
        at = one_hot(c == r * 8 + 4 * parity)
        values = dot(at, got[:, PAIRS * dq :], ((1,), (0,)))
        for p in range(PAIRS):
            by_slot = jnp.where(code == 2.0 * p + parity + 1.0, values[:, p : p + 1], by_slot)
    e = iota((EXPERTS, tok), 0)
    rows = []
    for k in range(k_top):
        named = jnp.broadcast_to(ids[k : k + 1, :], (EXPERTS, tok)) == e
        rows.append(jnp.sum(jnp.where(named, by_slot, 0.0), axis=0, keepdims=True))
    gate_grad[...] = (jnp.concatenate(rows, axis=0) / gates[...].astype(F32)).astype(BF)


def finish(ids, gates, got, d):
    out = (ids.shape[1], d)
    ins = (ids, gates, got)
    return pl.pallas_call(
        finish_kernel,
        grid=(1,),
        out_shape=[jax.ShapeDtypeStruct(out, BF), jax.ShapeDtypeStruct(ids.shape, BF)],
        in_specs=[whole(v.shape) for v in ins],
        out_specs=[whole(out), whole(ids.shape)],
        compiler_params=pltpu.CompilerParams(vmem_limit_bytes=24 * MIB),
        cost_estimate=cost(1 << 28, 2 * MIB),
        name="finish",
    )(*ins)


def swap(v, by):
    return lax.ppermute(v, "dp", [(i, i ^ by) for i in range(4)])


def exchange(v):
    shape = (EXPERTS, v.shape[0] // EXPERTS, v.shape[1])
    return lax.all_to_all(v.reshape(shape), "expert", split_axis=0, concat_axis=0, tiled=True).reshape(v.shape)


def plus(a, b):
    return (a.astype(F32) + b.astype(F32)).astype(BF)


def per_device(tokens, grad_out, expert_ids, gate_values, w_gate, w_up, w_down):
    features = tokens.shape[1]
    place = lax.axis_index("dp").astype(I32).reshape(1)
    ids, gates = expert_ids.T, gate_values.T
    wg, wu, wd = w_gate[0], w_up[0], w_down[0]
    got = exchange(pack(ids, gates, tokens, grad_out))
    far1, far3, near1, near3, back, x, s, h4, g = main_rows(place, got, wg, wu, wd)
    far1, far3 = swap(far1, 1), swap(far3, 3)
    near1, near3 = swap(near1, 1), swap(near3, 3)
    back = exchange(back)
    next1, next3, own1, own3 = next_parts(place, x, s, h4, g, far1, far3)
    next1, next3 = swap(next1, 3), swap(next3, 1)
    kept = plus(own1, near1), plus(own3, near3)
    token_grad, gate_grad = finish(ids, gates, back, features)
    kept, token_grad = lax.optimization_barrier((kept, token_grad))
    gate_wg, up_wg, down_wg = close(kept, (next1, next3), features)
    return (token_grad, gate_grad.T, gate_wg[None], up_wg[None], down_wg[None])


def solution(mesh):
    tok = P(("dp", "expert"), None)
    weight = P("expert", None, None)
    grad = P("expert", "dp", None)
    return jax.shard_map(
        per_device,
        mesh=mesh,
        in_specs=(tok, tok, tok, tok, weight, weight, weight),
        out_specs=(tok, tok, grad, grad, grad),
        check_vma=False,
    )
```

```python
import functools

import jax
import jax.numpy as jnp
from jax import lax
from jax.experimental import pallas as pl
from jax.experimental.pallas import tpu as pltpu
from jax.sharding import PartitionSpec as P

BF = jnp.bfloat16
F32 = jnp.float32
I32 = jnp.int32
CAP = 6
PAIRS = CAP // 2
EXPERTS = 64
EXT = 128
ROWS = EXPERTS * CAP
MIB = 1 << 20
SMEM_SPEC = pl.BlockSpec(memory_space=pltpu.SMEM)


def dot(a, b, dims):
    return lax.dot_general(a, b, (dims, ((), ())), preferred_element_type=F32)


def cost(flops, nbytes):
    return pl.CostEstimate(flops=flops, bytes_accessed=nbytes, transcendentals=0)


def whole(shape):
    return pl.BlockSpec(shape, lambda i: (0,) * len(shape))


def params():
    return pltpu.CompilerParams(vmem_limit_bytes=58 * MIB)


ANY_SPEC = pl.BlockSpec(memory_space=pl.ANY)


def fixed(x):
    return pltpu.with_memory_space_constraint(x, pltpu.HBM)


def iota(shape, dim):
    return lax.broadcasted_iota(I32, shape, dim)


def one_hot(hit):
    return jnp.where(hit, 1.0, 0.0).astype(BF)


def router(ids, gates, wide):
    k_top, tok = ids.shape
    rep = one_hot(iota((tok, wide), 0) == (iota((tok, wide), 1) & (tok - 1)))
    named_by = dot(ids[...].astype(F32).astype(BF), rep, ((1,), (0,)))
    gate_by = dot(gates[...], rep, ((1,), (0,)))
    shape = (EXPERTS, wide)
    e = iota(shape, 0).astype(F32)
    chosen = jnp.zeros(shape, F32)
    gate = jnp.zeros(shape, F32)
    for k in range(k_top):
        named = jnp.broadcast_to(named_by[k : k + 1, :], shape) == e
        chosen = jnp.where(named, 1.0, chosen)
        gate = jnp.where(named, jnp.broadcast_to(gate_by[k : k + 1, :], shape), gate)
    r, c = iota((wide, wide), 0), iota((wide, wide), 1)
    slot = dot(chosen.astype(BF), one_hot((r < c) & ((r >> 5) == (c >> 5))), ((1,), (0,)))
    return jnp.where(chosen > 0.0, slot + 1.0, 0.0), gate


def pack_kernel(ids, gates, tokens, grads, packed):
    tok, d = tokens.shape
    dq = d // 4
    wide = 8 * tok
    code, gate = router(ids, gates, wide)
    rows = packed.shape[0]
    own = one_hot((iota((rows, EXPERTS), 0) >> 4) == iota((rows, EXPERTS), 1))
    code = dot(own, code.astype(BF), ((1,), (0,)))
    gate = dot(own, gate.astype(BF), ((1,), (0,)))
    r, c = iota((rows, wide), 0), iota((rows, wide), 1)
    fits = (((r >> 3) & 1) == (c >> 7)) & ((r & 3) == ((c >> 5) & 3))
    value = jnp.where(c < 4 * tok, 1.0, gate)
    base = (((r >> 2) & 1) + 1).astype(F32)
    parts = [v[:, k * dq : (k + 1) * dq] for v in (tokens, grads) for k in range(4)]
    source = jnp.concatenate(parts, axis=0)
    for p in range(PAIRS):
        pick = jnp.where(fits & (code == base + 2.0 * p), value, 0.0).astype(BF)
        packed[:, p * dq : (p + 1) * dq] = dot(pick, source, ((1,), (0,))).astype(BF)


def pack(ids, gates, tokens, grads):
    tok, d = tokens.shape
    shape = (EXPERTS * 16, CAP * d // 8)
    ins = (ids, gates, tokens, grads)
    return pl.pallas_call(
        pack_kernel,
        grid=(1,),
        out_shape=pltpu.HBM(shape, BF),
        in_specs=[whole(v.shape) for v in ins],
        out_specs=whole(shape),
        compiler_params=params(),
        cost_estimate=cost(1 << 30, 4 * MIB),
        name="pack",
    )(*ins)


def put_down(ref, part, fq, width):
    top = ref.shape[0] - fq * 4 // 3
    third = fq // 3
    ref[top : top + fq, :] = part[:, :width]
    for i in range(3):
        cols = slice(i * width // 3, (i + 1) * width // 3)
        ref[top + fq :, cols] = part[i * third : (i + 1) * third, width:]


def gradient_part(ref, me, by, half, x_ref, s_ref, h4, g_ref):
    dq = x_ref.shape[1] // 4
    ff = g_ref.shape[1] // 2
    hd = s_ref.shape[1] // 2
    xq = x_ref[:, pl.ds(pl.multiple_of((me ^ by) * dq, dq), dq)]
    ref[:dq, :] = dot(xq, g_ref[:, half * ff : (half + 1) * ff], ((0,), (0,))).astype(BF)
    down = dot(h4[me ^ by], s_ref[:, half * hd : (half + 1) * hd], ((0,), (0,))).astype(BF)
    put_down(ref, down, h4.shape[2], ff)


def staged(refs, n_in, n_out):
    hbm_in, hbm_out = refs[:n_in], refs[n_in : n_in + n_out]
    vmem_in = refs[n_in + n_out : 2 * n_in + n_out]
    vmem_out = refs[2 * n_in + n_out : 2 * (n_in + n_out)]
    sems_in, sems_out = refs[2 * (n_in + n_out) :]
    loads = [pltpu.make_async_copy(h, v, sems_in.at[i]) for i, (h, v) in enumerate(zip(hbm_in, vmem_in))]
    stores = [pltpu.make_async_copy(v, h, sems_out.at[i]) for i, (h, v) in enumerate(zip(hbm_out, vmem_out))]
    for load in loads:
        load.start()
    return vmem_in, vmem_out, loads, stores


def staged_call(kernel, place, ins, shapes, limit, estimate, name):
    return pl.pallas_call(
        kernel,
        grid=(1,),
        out_shape=[pltpu.HBM(v, BF) for v in shapes],
        in_specs=[SMEM_SPEC] + [ANY_SPEC] * len(ins),
        out_specs=[ANY_SPEC] * len(shapes),
        scratch_shapes=[pltpu.VMEM(v.shape, BF) for v in ins]
        + [pltpu.VMEM(v, BF) for v in shapes]
        + [pltpu.SemaphoreType.DMA((len(ins),)), pltpu.SemaphoreType.DMA((len(shapes),))],
        compiler_params=pltpu.CompilerParams(vmem_limit_bytes=limit * MIB),
        cost_estimate=estimate,
        name=name,
    )(place, *ins)


def main_kernel(place, *refs):
    (got, wg, wu, wd), outs, loads, stores = staged(refs, 4, 9)
    back, x_ref, s_ref, h4, g_ref = outs[4:]
    d, ff = wg.shape
    dq, fq = d // 4, ff // 4
    o, c = iota((256, 256), 0), iota((256, 256), 1)
    i = o & 31
    unpick = one_hot(c == (i >> 1) * 16 + (o >> 7) * 8 + (i & 1) * 4 + ((o >> 5) & 3))
    loads[0].wait()
    for p in range(PAIRS):
        for b in range(4):
            part = dot(unpick, got[b * 256 : (b + 1) * 256, p * dq : (p + 1) * dq], ((1,), (0,))).astype(BF)
            rows = slice(p * 128 + b * 32, p * 128 + (b + 1) * 32)
            for k in range(4):
                x_ref[rows, k * dq : (k + 1) * dq] = part[k * 32 : (k + 1) * 32]
                s_ref[rows, k * dq : (k + 1) * dq] = part[128 + k * 32 : 128 + (k + 1) * 32]
    stores[5].start()
    stores[6].start()
    x = x_ref[...]
    loads[1].wait()
    a = dot(x, wg[...], ((1,), (0,)))
    loads[2].wait()
    u = dot(x, wu[...], ((1,), (0,)))
    loads[3].wait()
    gh = dot(s_ref[...], wd[...], ((1,), (1,)))
    sig = jax.nn.sigmoid(a)
    swish = a * sig
    hidden = (swish * u).astype(BF)
    g_ref[:, :ff] = (gh * (u * sig * (1.0 + a * (1.0 - sig)))).astype(BF)
    g_ref[:, ff:] = (gh * swish).astype(BF)
    for k in range(4):
        h4[k] = hidden[:, k * fq : (k + 1) * fq]
    stores[7].start()
    stores[8].start()
    me = place[0]
    far = me ^ 2
    xq = x_ref[:, pl.ds(pl.multiple_of(far * dq, dq), dq)]
    both = dot(xq, g_ref[...], ((0,), (0,))).astype(BF)
    down = dot(h4[far], s_ref[...], ((0,), (0,))).astype(BF)
    for n in range(2):
        outs[n][:dq, :] = both[:, n * ff : (n + 1) * ff]
        put_down(outs[n], down[:, n * d // 2 : (n + 1) * d // 2], fq, ff)
        stores[n].start()
    for n, by, half in ((2, 1, 0), (3, 3, 1)):
        gradient_part(outs[n], me, by, half, x_ref, s_ref, h4, g_ref)
        stores[n].start()
    total = jnp.sum(gh * hidden.astype(F32), axis=1, keepdims=True)
    o, c = iota((128, 128), 0), iota((128, 128), 1)
    repick = one_hot(c == (o & 3) * 32 + (o >> 3) * 2 + ((o >> 2) & 1))
    parts = []
    for k in range(4):
        cols = slice(k * dq, (k + 1) * dq)
        part = dot(g_ref[:, :ff], wg[cols, :], ((1,), (1,))) + dot(g_ref[:, ff:], wu[cols, :], ((1,), (1,)))
        parts.append(part.astype(BF))
    for p in range(PAIRS):
        for b in range(4):
            rows = slice(p * 128 + b * 32, p * 128 + (b + 1) * 32)
            four = jnp.concatenate([part[rows] for part in parts], axis=0)
            back[b * 128 : (b + 1) * 128, p * dq : (p + 1) * dq] = dot(repick, four, ((1,), (0,))).astype(BF)
    lane = iota((128, EXT), 1)
    mixed = jnp.zeros((128, EXT), F32)
    for p in range(PAIRS):
        mixed = jnp.where(lane == p, total[p * 128 : (p + 1) * 128], mixed)
    o, c = iota((512, 128), 0), iota((512, 128), 1)
    spread = one_hot((c == (o >> 3) * 2 + ((o >> 2) & 1)) & ((o & 3) == 0))
    back[:, PAIRS * dq :] = dot(spread, mixed.astype(BF), ((1,), (0,))).astype(BF)
    stores[4].start()
    for store in stores:
        store.wait()


def main_rows(place, got, wg, wu, wd):
    d, ff = wg.shape
    packed = (d // 4 + ff // 3, ff)
    shapes = [packed] * 4 + [(EXPERTS * 8, CAP * d // 8 + EXT)]
    shapes += [(ROWS, d), (ROWS, d), (4, ROWS, ff // 4), (ROWS, 2 * ff)]
    ins = (got, fixed(wg), fixed(wu), fixed(wd))
    return staged_call(main_kernel, place, ins, shapes, 46, cost(14 * ROWS * d * ff, 24 * MIB), "main_rows")


def next_kernel(place, *refs):
    (x_ref, s_ref, h4, g_ref, far1, far3), outs, loads, stores = staged(refs, 6, 4)
    for load in loads:
        load.wait()
    me = place[0]
    for n, by, half, got in ((0, 3, 0, far1), (1, 1, 1, far3), (2, 0, 0, None), (3, 0, 1, None)):
        gradient_part(outs[n], me, by, half, x_ref, s_ref, h4, g_ref)
        if got is not None:
            outs[n][...] = (outs[n][...].astype(F32) + got[...].astype(F32)).astype(BF)
        stores[n].start()
    for store in stores:
        store.wait()


def next_parts(place, x, s, h4, g, far1, far3):
    ins = (x, s, h4, g, far1, far3)
    estimate = cost(60 * ROWS * x.shape[1] * g.shape[1] // 2, 13 * MIB)
    return staged_call(next_kernel, place, ins, [far1.shape] * 4, 58, estimate, "next_parts")


def close_kernel(kept1, kept3, next1, next3, gate, up, down):
    dq, ff = gate.shape
    fq, d = down.shape
    third = fq // 3
    for half, (kept, got, out) in enumerate(((kept1, next1, gate), (kept3, next3, up))):
        total = (kept[...].astype(F32) + got[...].astype(F32)).astype(BF)
        out[...] = total[:dq]
        left = half * d // 2
        down[:, left : left + ff] = total[dq : dq + fq]
        for i in range(3):
            cols = slice(i * ff // 3, (i + 1) * ff // 3)
            down[i * third : (i + 1) * third, left + ff : left + d // 2] = total[dq + fq :, cols]


def close(kept, nexts, d):
    rows, ff = kept[0].shape
    shapes = [(d // 4, ff)] * 2 + [(ff // 4, d)]
    ins = (*kept, *nexts)
    return pl.pallas_call(
        close_kernel,
        grid=(1,),
        out_shape=[jax.ShapeDtypeStruct(v, BF) for v in shapes],
        in_specs=[whole(v.shape) for v in ins],
        out_specs=[whole(v) for v in shapes],
        compiler_params=pltpu.CompilerParams(vmem_limit_bytes=24 * MIB),
        cost_estimate=cost(1 << 21, 7 * MIB),
        name="close",
    )(*ins)


def finish_kernel(ids, gates, got, token_grad, gate_grad):
    k_top, tok = ids.shape
    wide = 4 * tok
    dq = token_grad.shape[1] // 4
    n = got.shape[0]
    code, _ = router(ids, gates, wide)
    from_e = one_hot(iota((EXPERTS, n), 0) == (iota((EXPERTS, n), 1) >> 3))
    code_cols = dot(code.astype(BF), from_e, ((0,), (0,)))
    r, c = iota((wide, n), 0), iota((wide, n), 1)
    fits = (r >> 5) == (c & 3)
    base = (((c >> 2) & 1) + 1).astype(F32)
    total = None
    for p in range(PAIRS):
        pick = one_hot(fits & (code_cols == base + 2.0 * p))
        part = dot(pick, got[:, p * dq : (p + 1) * dq], ((1,), (0,)))
        total = part if total is None else total + part
    for k in range(4):
        token_grad[:, k * dq : (k + 1) * dq] = total[k * tok : (k + 1) * tok].astype(BF)

    code = code[:, :tok]
    by_slot = jnp.zeros((EXPERTS, tok), F32)
    r, c = iota((EXPERTS, n), 0), iota((EXPERTS, n), 1)
    for parity in range(2):
        at = one_hot(c == r * 8 + 4 * parity)
        values = dot(at, got[:, PAIRS * dq :], ((1,), (0,)))
        for p in range(PAIRS):
            by_slot = jnp.where(code == 2.0 * p + parity + 1.0, values[:, p : p + 1], by_slot)
    e = iota((EXPERTS, tok), 0)
    rows = []
    for k in range(k_top):
        named = jnp.broadcast_to(ids[k : k + 1, :], (EXPERTS, tok)) == e
        rows.append(jnp.sum(jnp.where(named, by_slot, 0.0), axis=0, keepdims=True))
    gate_grad[...] = (jnp.concatenate(rows, axis=0) / gates[...].astype(F32)).astype(BF)


def finish(ids, gates, got, d):
    out = (ids.shape[1], d)
    ins = (ids, gates, got)
    return pl.pallas_call(
        finish_kernel,
        grid=(1,),
        out_shape=[jax.ShapeDtypeStruct(out, BF), jax.ShapeDtypeStruct(ids.shape, BF)],
        in_specs=[whole(v.shape) for v in ins],
        out_specs=[whole(out), whole(ids.shape)],
        compiler_params=pltpu.CompilerParams(vmem_limit_bytes=24 * MIB),
        cost_estimate=cost(1 << 28, 2 * MIB),
        name="finish",
    )(*ins)


def swap(v, by):
    return lax.ppermute(v, "dp", [(i, i ^ by) for i in range(4)])


def exchange(v):
    shape = (EXPERTS, v.shape[0] // EXPERTS, v.shape[1])
    return lax.all_to_all(v.reshape(shape), "expert", split_axis=0, concat_axis=0, tiled=True).reshape(v.shape)


def plus(a, b):
    return (a.astype(F32) + b.astype(F32)).astype(BF)


def per_device(tokens, grad_out, expert_ids, gate_values, w_gate, w_up, w_down):
    features = tokens.shape[1]
    place = lax.axis_index("dp").astype(I32).reshape(1)
    ids, gates = expert_ids.T, gate_values.T
    wg, wu, wd = w_gate[0], w_up[0], w_down[0]
    got = exchange(pack(ids, gates, tokens, grad_out))
    far1, far3, near1, near3, back, x, s, h4, g = main_rows(place, got, wg, wu, wd)
    far1, far3 = swap(far1, 1), swap(far3, 3)
    near1, near3 = swap(near1, 1), swap(near3, 3)
    back = exchange(back)
    next1, next3, own1, own3 = next_parts(place, x, s, h4, g, far1, far3)
    next1, next3 = swap(next1, 3), swap(next3, 1)
    kept = plus(own1, near1), plus(own3, near3)
    token_grad, gate_grad = finish(ids, gates, back, features)
    kept, token_grad = lax.optimization_barrier((kept, token_grad))
    gate_wg, up_wg, down_wg = close(kept, (next1, next3), features)
    return (token_grad, gate_grad.T, gate_wg[None], up_wg[None], down_wg[None])


def solution(mesh):
    tok = P(("dp", "expert"), None)
    weight = P("expert", None, None)
    grad = P("expert", "dp", None)
    return jax.shard_map(
        per_device,
        mesh=mesh,
        in_specs=(tok, tok, tok, tok, weight, weight, weight),
        out_specs=(tok, tok, grad, grad, grad),
        check_vma=False,
    )
```
